512 devices in a mesh: sec: 4 (over z_hi, core), tile: 128 (over z_lo, x, y).
Axes of the slice: x: 4, y: 4, z: 16 (z_hi: 2, z_lo: 8; z = z_hi * 8 + z_lo), core: 2. Of those that a mesh axis runs over, the one named last changes fastest.
Arguments:
- state: float32 [4, 128, 65536], P('sec', None, 'tile'), may hold values from -6 to 6
- tendency: bfloat16 [4, 128, 65536], P('sec', None, 'tile'), may hold values from -4 to 4
- diffusion: bfloat16 [4, 128, 65536], P('sec', None, 'tile'), may hold values from 0.019897461 to 0.23925781
- mixing: float32 [4, 128, 128], P('sec')
- coupling: float32 [4, 128], P('sec'), may hold values from 0.05 to 0.4
- remap_index: int32 [4, 4, 65536], P('sec', None, 'tile'), may hold values from 0 to 1535, as said below
- remap_weight: float32 [4, 4, 65536], P('sec', None, 'tile'), may hold values from 0.1 to 0.4
- active_cols: int32 [4], replicated, may hold values from 256 to 512
- send_cols: int32 [2, 4, 128, 128, 4], P(None, 'sec', 'tile'), may hold values from 0 to 511
- occ_slot: int32 [2, 4, 8, 8192], P(None, 'sec', None, 'tile'), may hold values from 0 to 511
- occ_weight: float32 [2, 4, 8, 8192], P(None, 'sec', None, 'tile'), may hold values from 0.2 to 0.6
- occ_count: int32 [2, 4, 8192], P(None, 'sec', 'tile'), may hold values from 1 to 8
- refraction: float32 [4, 128, 128], P('sec'), may hold values from -0.5 to 0.5
- abel_matrix: float32 [128, 256], replicated
- observed: float32 [2, 8192, 256], P(None, ('sec', 'tile')), may hold values from -6 to 6
Outputs:
- final_state: float32 [4, 128, 65536], P('sec', None, 'tile')
- departures: float32 [2, 8192, 256], P(None, ('sec', 'tile'))
The draws below stay inside these ranges and needn't reach their ends.
Inputs may be any that keep to these rules, and one draw needn't show every extreme that they name: `remap_index`: for an atmosphere section the value is a column within the tile of the ocean section; for the last section, value // 512 is the atmosphere section and value % 512 the column within the tile.
All inputs are finite; a program needn't handle non-finite values.
Results may differ from the reference program's by a relative error of at most 0.00035.
Values sent between devices are 32-bit elements; how exact they have to be, the bound alone decides.
No kernel may reach another device: no remote copies, remote signals or barrier semaphores. Data moves between devices by JAX's collectives and lax.ppermute only.
A program may use at most 64 MiB of HBM per device.

```python
import math
import jax
import jax.numpy as jnp
from jax import lax

LEV = 128
COLS = 512
SUBS = 4
STEPS = 2
RK = 4
CAP = 4
TPMAX = 8
NB = 256
OQ = 16
SECTIONS = 4
TILES = 128
NCOL = 65536
OCC_TILE = 64
OCCS = 8192


def draw_mixing(key, part):
    key_diag, key_rest = jax.random.split(key)
    diagonal = jax.random.uniform(key_diag, (SECTIONS, LEV), jnp.float32, 0.5, 0.65)
    spread = jax.random.uniform(key_rest, (SECTIONS, LEV, LEV), jnp.float32, -1.0, 1.0) * (0.35 / (LEV - 1))
    unit_diag = jnp.eye(LEV, dtype=jnp.float32)[None]
    return spread * (1.0 - unit_diag) + unit_diag * diagonal[:, :, None]


def draw_remap_index(key, part):
    drawn = jax.random.randint(key, (SECTIONS, RK, NCOL), 0, (SECTIONS - 1) * COLS)
    ocean_rows = (jnp.arange(SECTIONS) == SECTIONS - 1)[:, None, None]
    return jnp.where(ocean_rows, drawn, drawn % COLS).astype(jnp.int32)


def draw_active_cols(key, part):
    mixed_key = jax.random.fold_in(key, part)
    key_order, key_value = jax.random.split(mixed_key)
    drawn = jax.random.randint(key_value, (SECTIONS,), COLS // 2, COLS + 1)
    order = jax.random.permutation(key_order, SECTIONS)
    drawn = jnp.where(order == 0, COLS, drawn)
    drawn = jnp.where(order == 1, COLS // 2, drawn)
    return drawn.astype(jnp.int32)


def draw_abel_matrix(key, part):
    entries = jax.random.uniform(key, (LEV, NB), jnp.float32, 0.5, 1.5)
    level_index = jnp.arange(LEV)[:, None]
    height_index = jnp.arange(NB)[None, :]
    above_height = level_index * NB <= (NB - 1 - height_index) * LEV
    return jnp.where(above_height, entries, 0.0) * (1.0 / math.sqrt(LEV))


def place_ends(values, key, least, high):
    place = [jax.random.randint(jax.random.fold_in(key, axis), (), 0, length) for axis, length in enumerate(values.shape)]
    widest = values.shape.index(max(values.shape))
    neighbour = place[:widest] + [(place[widest] + 1) % values.shape[widest]] + place[widest + 1:]
    return values.at[tuple(place)].set(least).at[tuple(neighbour)].set(high)


def levels(own_key, shape, shards, smallest, top_value):
    def one(axis_at, blocks):
        heights = jax.random.uniform(jax.random.fold_in(jax.random.fold_in(own_key, 6), axis_at), (blocks,), jnp.float32, smallest / len(shards), top_value / len(shards))
        return jnp.repeat(jnp.exp(heights), shape[axis_at] // blocks).reshape((-1,) + (1,) * (len(shape) - axis_at - 1))

    level = one(*shards[0])
    for cut in shards[1:]:
        level = level * one(*cut)
    return level


def bell_draw(rng, extent, deviation, most, cuts=(), kind=jnp.bfloat16):
    values = deviation * jax.random.normal(rng, extent, jnp.float32)
    if cuts:
        values = values * levels(rng, extent, cuts, -0.22, 0.18)
    return jnp.clip(values, -most, most).astype(kind)


def setup_inputs(seed: int = 0) -> dict:
    seeds = jax.random.split(jax.random.key(seed), 16)
    state = bell_draw(seeds[0], (SECTIONS, LEV, NCOL), 1.0, 6.0, ((0, 4), (2, 128)), jnp.float32)
    tendency = bell_draw(seeds[1], (SECTIONS, LEV, NCOL), 0.3, 4.0, ((0, 4), (2, 128)))
    diffusion = jnp.clip(0.019897461 + 0.21936035 * jax.random.uniform(seeds[2], (SECTIONS, LEV, NCOL), jnp.float32) ** levels(seeds[2], (SECTIONS, LEV, NCOL), ((0, 4), (2, 128)), -0.2, 0.2), 0.019897461, 0.23925781).astype(jnp.bfloat16)
    mixing = draw_mixing(jax.random.fold_in(seeds[15], 71), 0)
    coupling = jnp.clip(0.05 + 0.35 * jax.random.uniform(seeds[4], (SECTIONS, LEV), jnp.float32) ** levels(seeds[4], (SECTIONS, LEV), ((0, 4),), -0.2, 0.2), 0.05, 0.4)
    remap_index = draw_remap_index(jax.random.fold_in(seeds[15], 71), 0)
    remap_weight = jnp.clip(0.1 + 0.3 * jax.random.uniform(seeds[6], (SECTIONS, RK, NCOL), jnp.float32) ** levels(seeds[6], (SECTIONS, RK, NCOL), ((0, 4), (2, 128)), -0.2, 0.2), 0.1, 0.4)
    active_cols = draw_active_cols(jax.random.fold_in(seeds[15], 71), 0)
    send_cols = place_ends(jax.random.randint(seeds[8], (STEPS, SECTIONS, TILES, TILES, CAP), 0, COLS), jax.random.fold_in(seeds[8], 1), 0, COLS - 1).astype(jnp.int32)
    occ_slot = place_ends(jax.random.randint(seeds[9], (STEPS, SECTIONS, TPMAX, TILES * OCC_TILE), 0, TILES * CAP), jax.random.fold_in(seeds[9], 1), 0, (TILES * CAP) - 1).astype(jnp.int32)
    occ_weight = jnp.clip(0.2 + 0.400000021 * jax.random.uniform(seeds[10], (STEPS, SECTIONS, TPMAX, TILES * OCC_TILE), jnp.float32) ** levels(seeds[10], (STEPS, SECTIONS, TPMAX, TILES * OCC_TILE), ((1, 4), (3, 128)), -0.2, 0.2), 0.2, 0.6)
    occ_count = place_ends(jax.random.randint(seeds[11], (STEPS, SECTIONS, TILES * OCC_TILE), 1, TPMAX + 1), jax.random.fold_in(seeds[11], 1), 1, TPMAX).astype(jnp.int32)
    refraction = bell_draw(seeds[12], (SECTIONS, LEV, LEV), LEV ** -0.5, 0.5, ((0, 4),), jnp.float32)
    abel_matrix = draw_abel_matrix(jax.random.fold_in(seeds[15], 71), 0)
    observed = bell_draw(seeds[14], (STEPS, OCCS, NB), 1.0, 6.0, ((1, 512),), jnp.float32)
    return dict(state=state, tendency=tendency, diffusion=diffusion, mixing=mixing, coupling=coupling, remap_index=remap_index, remap_weight=remap_weight, active_cols=active_cols, send_cols=send_cols, occ_slot=occ_slot, occ_weight=occ_weight, occ_count=occ_count, refraction=refraction, abel_matrix=abel_matrix, observed=observed)


def observe(field, sent, slots, weights, counts, refraction, abel_matrix, observed_step):
    highest = lax.Precision.HIGHEST
    owner_tile = jnp.arange(TILES * OCC_TILE, dtype=jnp.int32) // OCC_TILE
    source_tile = slots // CAP
    slot_index = slots % CAP
    section_ids = jnp.arange(SECTIONS, dtype=jnp.int32)[:, None, None]
    column_ids = source_tile * COLS + sent[section_ids, source_tile, owner_tile[None, None, :], slot_index]
    values = field[section_ids, :, column_ids]
    tangent_live = jnp.arange(TPMAX, dtype=jnp.int32)[None, :, None] < counts[:, None, :]
    live_weight = jnp.where(tangent_live, weights, 0.0)
    profile = jnp.sum(live_weight[..., None] * values, axis=1)
    projected = jnp.einsum('snl,slm->snm', profile, refraction, precision=highest)
    bending = jnp.einsum('snm,mb->nb', projected, abel_matrix, precision=highest)
    bending = bending.reshape(TILES, SECTIONS, OQ, NB).transpose(1, 0, 2, 3).reshape(OCCS, NB)
    return observed_step - bending


def reference(state, tendency, diffusion, mixing, coupling, remap_index, remap_weight, active_cols, send_cols, occ_slot, occ_weight, occ_count, refraction, abel_matrix, observed):
    highest = lax.Precision.HIGHEST
    column_ids = jnp.arange(NCOL, dtype=jnp.int32)
    local_index = column_ids % COLS
    tile_base = (column_ids // COLS) * COLS
    live_mask = local_index[None, :] < active_cols[:, None]
    section_ids = jnp.arange(SECTIONS, dtype=jnp.int32)
    ocean_rows = (section_ids == SECTIONS - 1)[:, None, None]
    source_section = jnp.where(ocean_rows, remap_index // COLS, SECTIONS - 1).astype(jnp.int32)
    source_column = (tile_base[None, None, :] + jnp.where(ocean_rows, remap_index % COLS, remap_index)).astype(jnp.int32)
    rates = diffusion.astype(jnp.float32)
    forcing = tendency.astype(jnp.float32)
    field = state
    results = []
    for period in range(STEPS):
        surface = field[:, LEV - 1, :]
        picked = surface[source_section, source_column]
        boundary = jnp.sum(remap_weight * picked, axis=1) - surface
        for substep in range(SUBS):
            spread = field + rates * (jnp.roll(field, 1, 2) + jnp.roll(field, -1, 2) - 2.0 * field)
            stepped = jnp.einsum('sij,sjc->sic', mixing, spread, precision=highest)
            stepped = stepped + coupling[:, :, None] * boundary[:, None, :] + forcing
            field = jnp.where(live_mask[:, None, :], stepped, field)
        results.append(observe(field, send_cols[period], occ_slot[period], occ_weight[period], occ_count[period], refraction, abel_matrix, observed[period]))
    return field, jnp.stack(results)
```

```python
import jax
import jax.numpy as jnp
from jax import lax
from jax.experimental import pallas as pl
from jax.experimental.pallas import tpu as pltpu
from jax.sharding import PartitionSpec as P

SUBS = 4
STEPS = 2
HALO = 8
LANES = 128
AXES = ("sec", "tile")
f32 = jnp.float32
bf16 = jnp.bfloat16


def call(body, outs, *args, scratch=()):
    in_specs = [
        pl.BlockSpec(memory_space=pltpu.SMEM if a.ndim == 1 else pltpu.VMEM) for a in args
    ]
    single = not isinstance(outs, (tuple, list))
    specs = pl.BlockSpec(memory_space=pltpu.VMEM)
    return pl.pallas_call(
        body,
        out_shape=outs if single else tuple(outs),
        in_specs=in_specs,
        out_specs=specs if single else tuple(specs for _ in outs),
        scratch_shapes=list(scratch),
        compiler_params=pltpu.CompilerParams(vmem_limit_bytes=40 * 2**20),
    )(*args)


def halves(x):
    high = x.astype(bf16)
    return high, (x - high.astype(f32)).astype(bf16)


def left_operand(x):
    high, low = halves(x)
    return jnp.concatenate([high, high, low], axis=1)


def right_operand(x):
    high, low = halves(x)
    return jnp.concatenate([high, low, high], axis=0)


def matmul(left, right):
    return jnp.dot(left, right, preferred_element_type=f32)


def pick(table, position):
    lane = position & (LANES - 1)
    row = position >> 7
    out = jnp.zeros(position.shape, f32)
    for r, values in enumerate(table):
        source = jnp.broadcast_to(values, position.shape)
        found = jnp.take_along_axis(source, lane, axis=1, mode="promise_in_bounds")
        out = jnp.where(row == r, found, out)
    return out


def lane_ids(shape):
    return lax.broadcasted_iota(jnp.int32, shape, len(shape) - 1)


def pack_edges(first, last):
    lane = lane_ids(first.shape)
    return jnp.where(lane < HALO, first, pltpu.roll(last, 2 * HALO, 1))


def prepare(scalars, state, tendency, diffusion, index, weight, out):
    columns = state.shape[1]
    levels = state.shape[0]
    tail = columns - LANES
    offset = scalars[5]
    block = jnp.zeros((levels, LANES), f32)
    lane = lane_ids(block.shape)
    for i, ref in enumerate((state, diffusion, tendency)):
        edges = pack_edges(ref[:, :LANES].astype(f32), ref[:, tail:].astype(f32))
        if i:
            edges = pltpu.roll(edges, 2 * HALO * i, 1)
        inside = (lane >= 2 * HALO * i) & (lane < 2 * HALO * (i + 1))
        block = jnp.where(inside, edges, block)
    out[0:48, :] = block.T[0:48, :]
    for j in range(columns // LANES):
        out[48 + j : 49 + j, :] = state[levels - 1 : levels, j * LANES : (j + 1) * LANES]
    out[52:56, :] = pack_edges(weight[:, :LANES], weight[:, tail:])
    position = (index[...] + offset).astype(f32)
    out[56:60, :] = pack_edges(position[:, :LANES], position[:, tail:])
    out[60:64, :] = jnp.zeros((4, LANES), f32)


def edge_boundary(table, shared, surface_first, surface_last, source):
    position = shared[source, 56:60, :].astype(jnp.int32)
    picked = pick(table, position)
    partner = jnp.sum(shared[source, 52:56, :] * picked, axis=0, keepdims=True)
    return partner - pack_edges(surface_first, surface_last)


def own_boundary(table, index, weight, surface, offset, out):
    for j in range(out.shape[1] // LANES):
        cut = slice(j * LANES, (j + 1) * LANES)
        picked = pick(table, index[:, cut] + offset)
        partner = jnp.sum(weight[:, cut] * picked, axis=0, keepdims=True)
        out[:, cut] = partner - surface(j)


def couple_first(scalars, shared, index, weight, boundary, forward, backward):
    section, offset = scalars[0], scalars[5]
    table = [shared[s, r : r + 1, :] for s in range(shared.shape[0]) for r in range(48, 52)]
    own_boundary(
        table, index, weight, lambda j: shared[section, 48 + j : 49 + j, :], offset, boundary
    )
    for out, source, start in ((forward, scalars[2], HALO), (backward, scalars[3], 0)):
        for i in range(3):
            row = 2 * HALO * i + start
            out[HALO * i : HALO * (i + 1), :] = shared[source, row : row + HALO, :]
        edge = edge_boundary(
            table, shared, shared[source, 48:49, :], shared[source, 51:52, :], source
        )
        out[24:32, :] = jnp.broadcast_to(edge, (8, LANES))


def couple_second(scalars, surfaces, shared, index, weight, boundary, forward, backward):
    section, offset = scalars[0], scalars[5]
    table = [surfaces[s, r : r + 1, :] for s in range(surfaces.shape[0]) for r in range(4)]
    own_boundary(
        table, index, weight, lambda j: surfaces[section, j : j + 1, :], offset, boundary
    )
    for out, source in ((forward, scalars[2]), (backward, scalars[3])):
        edge = edge_boundary(
            table, shared, surfaces[source, 0:1, :], surfaces[source, 3:4, :], source
        )
        out[...] = jnp.broadcast_to(edge, out.shape)


def edge_row(left, right):
    lane = lane_ids(left.shape)
    value = jnp.where(lane < HALO, right, 0.0)
    return jnp.where(lane >= LANES - HALO, pltpu.roll(left, LANES - 2 * HALO, 1), value)


def edge_block(left, right):
    gap = jnp.zeros((LANES - 2 * HALO, left.shape[1]), f32)
    return jnp.concatenate([right, gap, left], axis=0).T


def advance(field, rates, constant, mixing, live_limit):
    width = field.shape[1]
    lane = lane_ids((1, width))
    columns = width - LANES
    column = jnp.where(lane < columns, lane, lane - columns)
    column = jnp.where(lane < width - HALO, column, lane - LANES)
    live = column < live_limit
    left = left_operand(mixing)
    for _ in range(SUBS):
        near = pltpu.roll(field, 1, 1) + pltpu.roll(field, width - 1, 1)
        spread = field + rates * (near - 2.0 * field)
        stepped = matmul(left, right_operand(spread)) + constant
        field = jnp.where(live, stepped, field)
    return field


def forcing(coupling, boundary, edge, tendency):
    response = jnp.broadcast_to(coupling[...], (LANES, coupling.shape[1])).T
    row = jnp.concatenate([boundary[...], edge], axis=1)
    width = row.shape[1]
    parts = [
        response * row[:, j * LANES : (j + 1) * LANES] for j in range(width // LANES)
    ]
    return jnp.concatenate(parts, axis=1) + tendency


def chosen(field, listed):
    columns = field.shape[1] - LANES
    high, low = halves(field[:, :columns])
    stack = jnp.concatenate([high, low], axis=0)
    out = []
    for m in range(listed.shape[0]):
        row = listed[m : m + 1, :]
        column = lax.broadcasted_iota(jnp.int32, (columns, row.shape[1]), 0)
        hit = jnp.where(column == row, 1.0, 0.0).astype(bf16)
        both = matmul(stack, hit)
        levels = field.shape[0]
        out.append((both[:levels] + both[levels:]).T)
    return out


def step_first(
    scalars, state, tendency, diffusion, mixing, coupling, boundary, low, high, listed,
    window, rates_out, forcing_out, surface, parcel,
):
    rates = jnp.concatenate(
        [diffusion[...].astype(f32), edge_block(low[8:16, :], high[8:16, :])], axis=1
    )
    tend = jnp.concatenate(
        [tendency[...].astype(f32), edge_block(low[16:24, :], high[16:24, :])], axis=1
    )
    field = jnp.concatenate([state[...], edge_block(low[0:8, :], high[0:8, :])], axis=1)
    constant = forcing(coupling, boundary, edge_row(low[24:25, :], high[24:25, :]), tend)
    rates_out[...] = rates
    forcing_out[...] = tend
    field = advance(field, rates, constant, mixing[...], scalars[4])
    window[...] = field
    levels = field.shape[0]
    for j in range(4):
        surface[j : j + 1, :] = field[levels - 1 : levels, j * LANES : (j + 1) * LANES]
    for m, rows in enumerate(chosen(field, listed[0])):
        parcel[m] = rows


def step_second(
    scalars, window, rates, tend, mixing, coupling, boundary, low, high, listed, earlier,
    final, parcels,
):
    edge = edge_row(low[0:1, :], high[0:1, :])
    constant = forcing(coupling, boundary, edge, tend[...])
    field = advance(window[...], rates[...], constant, mixing[...], scalars[4])
    final[...] = field[:, : final.shape[1]]
    slots = earlier.shape[0]
    tiles = earlier.shape[1]
    for m in range(slots):
        parcels[pl.ds(m, tiles, stride=2 * slots), :] = earlier[m]
    for m, rows in enumerate(chosen(field, listed[1])):
        parcels[pl.ds(slots + m, tiles, stride=2 * slots), :] = rows


def weigh(slots, weights, counts, out):
    steps, ranks, occultations = slots.shape
    width = out.shape[2]
    tiles = width // 4
    for p in range(steps):
        rank = lax.broadcasted_iota(jnp.int32, (ranks, occultations), 0)
        live = jnp.where(rank < counts[p : p + 1, :], weights[p], 0.0).T
        key = ((slots[p] & 3) * tiles + (slots[p] >> 2)).T
        place = lane_ids((occultations, width))
        total = jnp.zeros((occultations, width), f32)
        for k in range(ranks):
            total = total + jnp.where(key[:, k : k + 1] == place, live[:, k : k + 1], 0.0)
        out[p] = total


def project(arrived, spread, refraction, out):
    steps, occultations, width = spread.shape
    tiles = width // 4
    owners = out.shape[0]
    rows = occultations // owners
    profiles = []
    for p in range(steps):
        values = jnp.concatenate(
            [arrived[pl.ds(4 * p + m, tiles, stride=4 * steps), :] for m in range(4)], axis=0
        )
        profiles.append(matmul(left_operand(spread[p]), right_operand(values)))
    profile = jnp.concatenate(profiles, axis=0)
    projected = matmul(left_operand(profile), right_operand(refraction[...]))
    for p in range(steps):
        for q in range(owners):
            start = p * occultations + q * rows
            out[q, p * rows : (p + 1) * rows, :] = projected[start : start + rows, :]


def depart(received, abel, observed, out):
    total = received[0]
    for s in range(1, received.shape[0]):
        total = total + received[s]
    bending = matmul(left_operand(total), right_operand(abel[...]))
    steps, rows, _ = observed.shape
    for p in range(steps):
        out[p] = observed[p] - bending[p * rows : (p + 1) * rows, :]


def shards(
    state,
    tendency,
    diffusion,
    mixing,
    coupling,
    remap_index,
    remap_weight,
    active_cols,
    send_cols,
    occ_slot,
    occ_weight,
    occ_count,
    refraction,
    abel_matrix,
    observed,
):
    section = lax.axis_index("sec")
    tile = lax.axis_index("tile")
    sections = lax.axis_size("sec")
    tiles = lax.axis_size("tile")
    levels, columns = state.shape[1:]
    half = sections // 2
    other = (section + half) % sections
    scalars = jnp.stack(
        [
            section,
            tile,
            jnp.where(tile == tiles - 1, other, section),
            jnp.where(tile == 0, other, section),
            lax.dynamic_index_in_dim(active_cols, section, 0, keepdims=False),
            jnp.where(section == sections - 1, 0, (sections - 1) * columns),
        ]
    ).astype(jnp.int32)
    forward = []
    for s in range(sections):
        for t in range(tiles):
            seam = t == tiles - 1
            target = ((s + half) % sections if seam else s) * tiles + (t + 1) % tiles
            forward.append((s * tiles + t, target))
    backward = [(target, source) for source, target in forward]
    listed = jnp.transpose(send_cols[:, 0, 0], (0, 2, 1))
    index, weight = remap_index[0], remap_weight[0]
    shape = jax.ShapeDtypeStruct
    width = columns + LANES

    edges = call(
        prepare, shape((64, LANES), f32), scalars, state[0], tendency[0], diffusion[0], index, weight
    )
    shared = lax.all_gather(edges, "sec", axis=0, tiled=False)
    boundary, up, down = call(
        couple_first,
        (shape((1, columns), f32), shape((32, LANES), f32), shape((32, LANES), f32)),
        scalars, shared, index, weight,
    )
    low = lax.ppermute(up, AXES, forward)
    high = lax.ppermute(down, AXES, backward)
    spread = call(
        weigh,
        shape((STEPS, occ_slot.shape[3], 4 * tiles), f32),
        occ_slot[:, 0], occ_weight[:, 0], occ_count[:, 0],
    )
    window, rates, tend, surface, parcel = call(
        step_first,
        (
            shape((levels, width), f32),
            shape((levels, width), f32),
            shape((levels, width), f32),
            shape((4, LANES), f32),
            shape((4, tiles, levels), f32),
        ),
        scalars, state[0], tendency[0], diffusion[0], mixing[0], coupling, boundary, low, high, listed,
    )
    surfaces = lax.all_gather(surface, "sec", axis=0, tiled=False)
    boundary, up, down = call(
        couple_second,
        (shape((1, columns), f32), shape((8, LANES), f32), shape((8, LANES), f32)),
        scalars, surfaces, shared, index, weight,
    )
    low = lax.ppermute(up, AXES, forward)
    high = lax.ppermute(down, AXES, backward)
    final, parcels = call(
        step_second,
        (shape((levels, columns), f32), shape((8 * tiles, levels), f32)),
        scalars, window, rates, tend, mixing[0], coupling, boundary, low, high, listed, parcel,
    )
    arrived = lax.all_to_all(
        parcels.reshape(tiles, 8, levels), "tile", split_axis=0, concat_axis=0, tiled=True
    )
    rows = observed.shape[1]
    partial = call(
        project,
        shape((sections, STEPS * rows, levels), f32),
        arrived.reshape(8 * tiles, levels), spread, refraction[0],
    )
    received = lax.all_to_all(partial, "sec", split_axis=0, concat_axis=0, tiled=True)
    departures = call(
        depart, shape((STEPS, rows, observed.shape[2]), f32), received, abel_matrix, observed
    )
    return (final[None], departures)


def solution(mesh):
    return jax.shard_map(
        shards,
        mesh=mesh,
        in_specs=(
            P("sec", None, "tile"),
            P("sec", None, "tile"),
            P("sec", None, "tile"),
            P("sec", None, None),
            P("sec", None),
            P("sec", None, "tile"),
            P("sec", None, "tile"),
            P(),
            P(None, "sec", "tile", None, None),
            P(None, "sec", None, "tile"),
            P(None, "sec", None, "tile"),
            P(None, "sec", "tile"),
            P("sec", None, None),
            P(),
            P(None, ("sec", "tile"), None),
        ),
        out_specs=(P("sec", None, "tile"), P(None, ("sec", "tile"), None)),
        check_vma=False,
    )
```

```python
import jax
import jax.numpy as jnp
from jax import lax
from jax.experimental import pallas as pl
from jax.experimental.pallas import tpu as pltpu
from jax.sharding import PartitionSpec as P

SUBS = 4
STEPS = 2
HALO = 8
LANES = 128
AXES = ("sec", "tile")
f32 = jnp.float32
bf16 = jnp.bfloat16


def call(body, outs, *args, scratch=(), space=pltpu.VMEM):
    in_specs = [
        pl.BlockSpec(memory_space=pltpu.SMEM if a.ndim == 1 else space) for a in args
    ]
    single = not isinstance(outs, (tuple, list))
    specs = pl.BlockSpec(memory_space=pltpu.VMEM)
    return pl.pallas_call(
        body,
        out_shape=outs if single else tuple(outs),
        in_specs=in_specs,
        out_specs=specs if single else tuple(specs for _ in outs),
        scratch_shapes=list(scratch),
        compiler_params=pltpu.CompilerParams(vmem_limit_bytes=40 * 2**20),
    )(*args)


def halves(x):
    high = x.astype(bf16)
    return high, (x - high.astype(f32)).astype(bf16)


def left_operand(x):
    high, low = halves(x)
    return jnp.concatenate([high, high, low], axis=1)


def right_operand(x):
    high, low = halves(x)
    return jnp.concatenate([high, low, high], axis=0)


def matmul(left, right):
    return jnp.dot(left, right, preferred_element_type=f32)


def pick(table, position):
    lane = position & (LANES - 1)
    row = position >> 7
    out = jnp.zeros(position.shape, f32)
    for r, values in enumerate(table):
        source = jnp.broadcast_to(values, position.shape)
        found = jnp.take_along_axis(source, lane, axis=1, mode="promise_in_bounds")
        out = jnp.where(row == r, found, out)
    return out


def position_offset(columns):
    ocean = lax.axis_size("sec") - 1
    return jnp.where(lax.axis_index("sec") == ocean, 0, ocean * columns)


def edge_sources():
    section, tile = lax.axis_index("sec"), lax.axis_index("tile")
    sections = lax.axis_size("sec")
    other = section + sections // 2
    other = jnp.where(other >= sections, other - sections, other)
    last = lax.axis_size("tile") - 1
    return jnp.where(tile == last, other, section), jnp.where(tile == 0, other, section)


def lane_ids(shape):
    return lax.broadcasted_iota(jnp.int32, shape, len(shape) - 1)


def pack_edges(first, last):
    lane = lane_ids(first.shape)
    return jnp.where(lane < HALO, first, pltpu.roll(last, 2 * HALO, 1))


def prepare(state, tendency, diffusion, index, weight, out, *scratch):
    levels, columns = state.shape
    tail = columns - LANES
    *ends, bottom, indices, weights, sems = scratch
    pairs = []
    for ref, head, back in zip((state, diffusion, tendency), ends[::2], ends[1::2]):
        pairs.append((ref.at[:, pl.ds(0, LANES)], head))
        pairs.append((ref.at[:, pl.ds(tail, LANES)], back))
    pairs.append((state.at[pl.ds(levels - 8, 8), :], bottom))
    pairs.append((index, indices))
    pairs.append((weight, weights))
    copies = [
        pltpu.make_async_copy(source, target, sems.at[i])
        for i, (source, target) in enumerate(pairs)
    ]
    for copy in copies:
        copy.start()
    for copy in copies:
        copy.wait()
    block = jnp.zeros((levels, LANES), f32)
    lane = lane_ids(block.shape)
    for i in range(3):
        edges = pack_edges(ends[2 * i][...].astype(f32), ends[2 * i + 1][...].astype(f32))
        if i:
            edges = pltpu.roll(edges, 2 * HALO * i, 1)
        inside = (lane >= 2 * HALO * i) & (lane < 2 * HALO * (i + 1))
        block = jnp.where(inside, edges, block)
    out[0:48, :] = block.T[0:48, :]
    for j in range(columns // LANES):
        out[48 + j : 49 + j, :] = bottom[7:8, j * LANES : (j + 1) * LANES]
    out[52:56, :] = pack_edges(weights[:, :LANES], weights[:, tail:])
    position = (indices[...] + position_offset(columns)).astype(f32)
    out[56:60, :] = pack_edges(position[:, :LANES], position[:, tail:])
    out[60:64, :] = jnp.zeros((4, LANES), f32)


def edge_boundary(table, shared, surface_first, surface_last, source):
    position = shared[source, 56:60, :].astype(jnp.int32)
    picked = pick(table, position)
    partner = jnp.sum(shared[source, 52:56, :] * picked, axis=0, keepdims=True)
    return partner - pack_edges(surface_first, surface_last)


def own_boundary(table, index, weight, surface, out):
    offset = position_offset(out.shape[1])
    for j in range(out.shape[1] // LANES):
        cut = slice(j * LANES, (j + 1) * LANES)
        picked = pick(table, index[:, cut] + offset)
        partner = jnp.sum(weight[:, cut] * picked, axis=0, keepdims=True)
        out[:, cut] = partner - surface(j)


def couple_first(shared, index, weight, boundary, forward, backward):
    section = lax.axis_index("sec")
    table = [shared[s, r : r + 1, :] for s in range(shared.shape[0]) for r in range(48, 52)]
    own_boundary(
        table, index, weight, lambda j: shared[section, 48 + j : 49 + j, :], boundary
    )
    for out, source, start in zip((forward, backward), edge_sources(), (HALO, 0)):
        for i in range(3):
            row = 2 * HALO * i + start
            out[HALO * i : HALO * (i + 1), :] = shared[source, row : row + HALO, :]
        edge = edge_boundary(
            table, shared, shared[source, 48:49, :], shared[source, 51:52, :], source
        )
        out[24:32, :] = jnp.broadcast_to(edge, (8, LANES))


def couple_second(surfaces, shared, index, weight, boundary, forward, backward):
    section = lax.axis_index("sec")
    table = [surfaces[s, r : r + 1, :] for s in range(surfaces.shape[0]) for r in range(4)]
    own_boundary(
        table, index, weight, lambda j: surfaces[section, j : j + 1, :], boundary
    )
    for out, source in zip((forward, backward), edge_sources()):
        edge = edge_boundary(
            table, shared, surfaces[source, 0:1, :], surfaces[source, 3:4, :], source
        )
        out[...] = jnp.broadcast_to(edge, out.shape)


def edge_row(left, right):
    lane = lane_ids(left.shape)
    value = jnp.where(lane < HALO, right, 0.0)
    return jnp.where(lane >= LANES - HALO, pltpu.roll(left, LANES - 2 * HALO, 1), value)


def edge_block(left, right):
    gap = jnp.zeros((LANES - 2 * HALO, left.shape[1]), f32)
    return jnp.concatenate([right, gap, left], axis=0).T


def advance(field, rates, constant, left, alive):
    width = field.shape[1]
    live = alive[...] > 0.0
    for _ in range(SUBS):
        near = pltpu.roll(field, 1, 1) + pltpu.roll(field, width - 1, 1)
        spread = field + rates * (near - 2.0 * field)
        stepped = matmul(left, right_operand(spread)) + constant
        field = jnp.where(live, stepped, field)
    return field


def forcing(response, boundary, edge, tendency):
    row = jnp.concatenate([boundary[...], edge], axis=1)
    width = row.shape[1]
    parts = [
        response * row[:, j * LANES : (j + 1) * LANES] for j in range(width // LANES)
    ]
    return jnp.concatenate(parts, axis=1) + tendency


def one_hot(listed, columns):
    row = jnp.concatenate([listed[m : m + 1, :] for m in range(listed.shape[0])], axis=1)
    column = lax.broadcasted_iota(jnp.int32, (columns, row.shape[1]), 0)
    return jnp.where(column == row, 1.0, 0.0).astype(bf16)


def chosen(field, hits):
    levels = field.shape[0]
    high, low = halves(field[:, : hits.shape[0]])
    both = matmul(jnp.concatenate([high, low], axis=0), hits[...])
    both = both[:levels] + both[levels:]
    tiles = hits.shape[1] // 4
    return [both[:, m * tiles : (m + 1) * tiles].T for m in range(4)]


def step_first(
    state, tendency, diffusion, left, response, alive, hits, boundary, low, high,
    window, rates_out, forcing_out, surface, parcel,
):
    rates = jnp.concatenate(
        [diffusion[...].astype(f32), edge_block(low[8:16, :], high[8:16, :])], axis=1
    )
    tend = jnp.concatenate(
        [tendency[...].astype(f32), edge_block(low[16:24, :], high[16:24, :])], axis=1
    )
    field = jnp.concatenate([state[...], edge_block(low[0:8, :], high[0:8, :])], axis=1)
    edge = edge_row(low[24:25, :], high[24:25, :])
    constant = forcing(response[...], boundary, edge, tend)
    rates_out[...] = rates
    forcing_out[...] = tend
    field = advance(field, rates, constant, left[...], alive)
    window[...] = field
    levels = field.shape[0]
    for j in range(4):
        surface[j : j + 1, :] = field[levels - 1 : levels, j * LANES : (j + 1) * LANES]
    for m, rows in enumerate(chosen(field, hits)):
        parcel[m] = rows


def step_second(
    window, rates, tend, left, response, alive, hits, boundary, low, high, earlier,
    final, parcels,
):
    edge = edge_row(low[0:1, :], high[0:1, :])
    constant = forcing(response[...], boundary, edge, tend[...])
    field = advance(window[...], rates[...], constant, left[...], alive)
    final[...] = field[:, : final.shape[1]]
    slots = earlier.shape[0]
    tiles = earlier.shape[1]
    for m in range(slots):
        parcels[pl.ds(m, tiles, stride=2 * slots), :] = earlier[m]
    for m, rows in enumerate(chosen(field, hits)):
        parcels[pl.ds(slots + m, tiles, stride=2 * slots), :] = rows


def ready_first(active, mixing, coupling, listed, left, response, alive, hits):
    width = alive.shape[1]
    lane = lane_ids((1, width))
    column = jnp.where(lane < width - LANES, lane, lane - (width - LANES))
    column = jnp.where(lane < width - HALO, column, lane - LANES)
    alive[...] = jnp.where(column < active[lax.axis_index("sec")], 1.0, 0.0)
    left[...] = left_operand(mixing[...])
    response[...] = jnp.broadcast_to(coupling[...], (LANES, coupling.shape[1])).T
    hits[...] = one_hot(listed[0], hits.shape[0])


def ready_second(listed, slots, weights, counts, refraction, abel, hits, spread, right, right_abel):
    hits[...] = one_hot(listed[1], hits.shape[0])
    right[...] = right_operand(refraction[...])
    right_abel[...] = right_operand(abel[...])
    steps, ranks, occultations = slots.shape
    width = spread.shape[2] // 3
    tiles = width // 4
    for p in range(steps):
        rank = lax.broadcasted_iota(jnp.int32, (ranks, occultations), 0)
        live = jnp.where(rank < counts[p : p + 1, :], weights[p], 0.0).T
        key = ((slots[p] & 3) * tiles + (slots[p] >> 2)).T
        place = lane_ids((occultations, width))
        total = jnp.zeros((occultations, width), f32)
        for k in range(ranks):
            total = total + jnp.where(key[:, k : k + 1] == place, live[:, k : k + 1], 0.0)
        spread[p] = left_operand(total)


def project(arrived, spread, refraction, out):
    steps, occultations, width = spread.shape
    tiles = width // 12
    owners = out.shape[0]
    rows = occultations // owners
    profiles = []
    for p in range(steps):
        values = jnp.concatenate(
            [arrived[pl.ds(4 * p + m, tiles, stride=4 * steps), :] for m in range(4)], axis=0
        )
        profiles.append(matmul(spread[p], right_operand(values)))
    profile = jnp.concatenate(profiles, axis=0)
    projected = matmul(left_operand(profile), refraction[...])
    for p in range(steps):
        for q in range(owners):
            start = p * occultations + q * rows
            out[q, p * rows : (p + 1) * rows, :] = projected[start : start + rows, :]


def depart(received, abel, observed, out):
    total = received[0]
    for s in range(1, received.shape[0]):
        total = total + received[s]
    bending = matmul(left_operand(total), abel[...])
    steps, rows, _ = observed.shape
    for p in range(steps):
        out[p] = observed[p] - bending[p * rows : (p + 1) * rows, :]


def shards(
    state,
    tendency,
    diffusion,
    mixing,
    coupling,
    remap_index,
    remap_weight,
    active_cols,
    send_cols,
    occ_slot,
    occ_weight,
    occ_count,
    refraction,
    abel_matrix,
    observed,
):
    sections = lax.axis_size("sec")
    tiles = lax.axis_size("tile")
    levels, columns = state.shape[1:]
    rows, heights = observed.shape[1:]
    width = columns + LANES
    half = sections // 2
    forward = []
    for s in range(sections):
        for t in range(tiles):
            seam = t == tiles - 1
            target = ((s + half) % sections if seam else s) * tiles + (t + 1) % tiles
            forward.append((s * tiles + t, target))
    backward = [(target, source) for source, target in forward]
    listed = jnp.transpose(send_cols[:, 0, 0], (0, 2, 1))
    index, weight = remap_index[0], remap_weight[0]
    shape = jax.ShapeDtypeStruct
    after = lax.optimization_barrier

    edges = call(
        prepare,
        shape((64, LANES), f32),
        *(
            pltpu.with_memory_space_constraint(x, pltpu.HBM)
            for x in (state[0], tendency[0], diffusion[0], index, weight)
        ),
        space=pltpu.HBM,
        scratch=[pltpu.VMEM((levels, LANES), f32)] * 2
        + [pltpu.VMEM((levels, LANES), bf16)] * 4
        + [
            pltpu.VMEM((8, columns), f32),
            pltpu.VMEM(index.shape, jnp.int32),
            pltpu.VMEM(weight.shape, f32),
            pltpu.SemaphoreType.DMA((9,)),
        ],
    )
    shared = lax.all_gather(edges, "sec", axis=0, tiled=False)
    boundary, up, down = call(
        couple_first,
        (shape((1, columns), f32), shape((32, LANES), f32), shape((32, LANES), f32)),
        shared, index, weight,
    )
    low = lax.ppermute(up, AXES, forward)
    high = lax.ppermute(down, AXES, backward)
    mixing_row, _ = after((mixing[0], boundary))
    left, response, alive, hits = call(
        ready_first,
        (
            shape((levels, 3 * levels), bf16),
            shape((levels, LANES), f32),
            shape((1, width), f32),
            shape((columns, 4 * tiles), bf16),
        ),
        active_cols, mixing_row, coupling, listed,
    )
    window, rates, tend, surface, parcel = call(
        step_first,
        (
            shape((levels, width), f32),
            shape((levels, width), f32),
            shape((levels, width), f32),
            shape((4, LANES), f32),
            shape((4, tiles, levels), f32),
        ),
        state[0], tendency[0], diffusion[0], left, response, alive, hits, boundary, low, high,
    )
    surfaces = lax.all_gather(surface, "sec", axis=0, tiled=False)
    boundary, up, down = call(
        couple_second,
        (shape((1, columns), f32), shape((8, LANES), f32), shape((8, LANES), f32)),
        surfaces, shared, index, weight,
    )
    low = lax.ppermute(up, AXES, forward)
    high = lax.ppermute(down, AXES, backward)
    weights, _ = after((occ_weight[:, 0], boundary))
    hits, spread, right, right_abel = call(
        ready_second,
        (
            shape((columns, 4 * tiles), bf16),
            shape((STEPS, occ_slot.shape[3], 12 * tiles), bf16),
            shape((3 * levels, levels), bf16),
            shape((3 * levels, heights), bf16),
        ),
        listed, occ_slot[:, 0], weights, occ_count[:, 0], refraction[0], abel_matrix,
    )
    final, parcels = call(
        step_second,
        (shape((levels, columns), f32), shape((8 * tiles, levels), f32)),
        window, rates, tend, left, response, alive, hits, boundary, low, high, parcel,
    )
    parcels, spread, right, right_abel, observed = after(
        (parcels, spread, right, right_abel, observed)
    )
    arrived = lax.all_to_all(
        parcels.reshape(tiles, 8, levels), "tile", split_axis=0, concat_axis=0, tiled=True
    )
    partial = call(
        project,
        shape((sections, STEPS * rows, levels), f32),
        arrived.reshape(8 * tiles, levels), spread, right,
    )
    received = lax.all_to_all(partial, "sec", split_axis=0, concat_axis=0, tiled=True)
    departures = call(
        depart, shape((STEPS, rows, heights), f32), received, right_abel, observed
    )
    return (final[None], departures)


def solution(mesh):
    return jax.shard_map(
        shards,
        mesh=mesh,
        in_specs=(
            P("sec", None, "tile"),
            P("sec", None, "tile"),
            P("sec", None, "tile"),
            P("sec", None, None),
            P("sec", None),
            P("sec", None, "tile"),
            P("sec", None, "tile"),
            P(),
            P(None, "sec", "tile", None, None),
            P(None, "sec", None, "tile"),
            P(None, "sec", None, "tile"),
            P(None, "sec", "tile"),
            P("sec", None, None),
            P(),
            P(None, ("sec", "tile"), None),
        ),
        out_specs=(P("sec", None, "tile"), P(None, ("sec", "tile"), None)),
        check_vma=False,
    )
```

```python
import jax
import jax.numpy as jnp
from jax import lax
from jax.experimental import pallas as pl
from jax.experimental.pallas import tpu as pltpu
from jax.sharding import PartitionSpec as P

SUBS = 4
STEPS = 2
HALO = 8
LANES = 128
AXES = ("sec", "tile")
f32 = jnp.float32
bf16 = jnp.bfloat16


def call(body, outs, *args, scratch=(), space=pltpu.VMEM):
    in_specs = [
        pl.BlockSpec(memory_space=pltpu.SMEM if a.ndim == 1 else space) for a in args
    ]
    single = not isinstance(outs, (tuple, list))
    specs = pl.BlockSpec(memory_space=pltpu.VMEM)
    return pl.pallas_call(
        body,
        out_shape=outs if single else tuple(outs),
        in_specs=in_specs,
        out_specs=specs if single else tuple(specs for _ in outs),
        scratch_shapes=list(scratch),
        compiler_params=pltpu.CompilerParams(vmem_limit_bytes=40 * 2**20),
    )(*args)


def halves(x):
    high = x.astype(bf16)
    return high, (x - high.astype(f32)).astype(bf16)


def left_operand(x):
    high, low = halves(x)
    return jnp.concatenate([high, high, low], axis=1)


def right_operand(x):
    high, low = halves(x)
    return jnp.concatenate([high, low, high], axis=0)


def matmul(left, right):
    return jnp.dot(left, right, preferred_element_type=f32)


def pick(table, position):
    lane = position & (LANES - 1)
    row = position >> 7
    out = jnp.zeros(position.shape, f32)
    for r, values in enumerate(table):
        source = jnp.broadcast_to(values, position.shape)
        found = jnp.take_along_axis(source, lane, axis=1, mode="promise_in_bounds")
        out = jnp.where(row == r, found, out)
    return out


def position_offset(columns):
    ocean = lax.axis_size("sec") - 1
    return jnp.where(lax.axis_index("sec") == ocean, 0, ocean * columns)


def edge_sources():
    section, tile = lax.axis_index("sec"), lax.axis_index("tile")
    sections = lax.axis_size("sec")
    other = section + sections // 2
    other = jnp.where(other >= sections, other - sections, other)
    last = lax.axis_size("tile") - 1
    return jnp.where(tile == last, other, section), jnp.where(tile == 0, other, section)


def even_tile():
    return lax.rem(lax.axis_index("tile"), 2) == 0


def sent_edges():
    up, down = edge_sources()
    even = even_tile()
    return (
        (jnp.where(even, down, up), jnp.where(even, 0, HALO)),
        (jnp.where(even, up, down), jnp.where(even, HALO, 0)),
    )


def sides(odd, even, start, rows):
    first, second = odd[start : start + rows, :], even[start : start + rows, :]
    here = even_tile()
    return jnp.where(here, first, second), jnp.where(here, second, first)


def lane_ids(shape):
    return lax.broadcasted_iota(jnp.int32, shape, len(shape) - 1)


def pack_edges(first, last):
    lane = lane_ids(first.shape)
    return jnp.where(lane < HALO, first, pltpu.roll(last, 2 * HALO, 1))


def prepare(state, tendency, diffusion, index, weight, out, *scratch):
    levels, columns = state.shape
    tail = columns - LANES
    *ends, bottom, indices, weights, sems = scratch
    pairs = []
    for ref, head, back in zip((state, diffusion, tendency), ends[::2], ends[1::2]):
        pairs.append((ref.at[:, pl.ds(0, LANES)], head))
        pairs.append((ref.at[:, pl.ds(tail, LANES)], back))
    pairs.append((state.at[pl.ds(levels - 8, 8), :], bottom))
    pairs.append((index, indices))
    pairs.append((weight, weights))
    copies = [
        pltpu.make_async_copy(source, target, sems.at[i])
        for i, (source, target) in enumerate(pairs)
    ]
    for copy in copies:
        copy.start()
    for copy in copies:
        copy.wait()
    block = jnp.zeros((levels, LANES), f32)
    lane = lane_ids(block.shape)
    for i in range(3):
        edges = pack_edges(ends[2 * i][...].astype(f32), ends[2 * i + 1][...].astype(f32))
        if i:
            edges = pltpu.roll(edges, 2 * HALO * i, 1)
        inside = (lane >= 2 * HALO * i) & (lane < 2 * HALO * (i + 1))
        block = jnp.where(inside, edges, block)
    out[0:48, :] = block.T[0:48, :]
    for j in range(columns // LANES):
        out[48 + j : 49 + j, :] = bottom[7:8, j * LANES : (j + 1) * LANES]
    out[52:56, :] = pack_edges(weights[:, :LANES], weights[:, tail:])
    position = (indices[...] + position_offset(columns)).astype(f32)
    out[56:60, :] = pack_edges(position[:, :LANES], position[:, tail:])
    out[60:64, :] = jnp.zeros((4, LANES), f32)


def edge_boundary(table, shared, surface_first, surface_last, source):
    position = shared[source, 56:60, :].astype(jnp.int32)
    picked = pick(table, position)
    partner = jnp.sum(shared[source, 52:56, :] * picked, axis=0, keepdims=True)
    return partner - pack_edges(surface_first, surface_last)


def own_boundary(table, index, weight, surface, out):
    offset = position_offset(out.shape[1])
    for j in range(out.shape[1] // LANES):
        cut = slice(j * LANES, (j + 1) * LANES)
        picked = pick(table, index[:, cut] + offset)
        partner = jnp.sum(weight[:, cut] * picked, axis=0, keepdims=True)
        out[:, cut] = partner - surface(j)


def couple_first(shared, index, weight, boundary, odd, even):
    section = lax.axis_index("sec")
    table = [shared[s, r : r + 1, :] for s in range(shared.shape[0]) for r in range(48, 52)]
    own_boundary(
        table, index, weight, lambda j: shared[section, 48 + j : 49 + j, :], boundary
    )
    for out, (source, start) in zip((odd, even), sent_edges()):
        for i in range(3):
            row = pl.multiple_of(2 * HALO * i + start, HALO)
            out[HALO * i : HALO * (i + 1), :] = shared[source, pl.ds(row, HALO), :]
        edge = edge_boundary(
            table, shared, shared[source, 48:49, :], shared[source, 51:52, :], source
        )
        out[24:32, :] = jnp.broadcast_to(edge, (8, LANES))


def couple_second(surfaces, shared, index, weight, boundary, odd, even):
    section = lax.axis_index("sec")
    table = [surfaces[s, r : r + 1, :] for s in range(surfaces.shape[0]) for r in range(4)]
    own_boundary(
        table, index, weight, lambda j: surfaces[section, j : j + 1, :], boundary
    )
    for out, (source, _) in zip((odd, even), sent_edges()):
        edge = edge_boundary(
            table, shared, surfaces[source, 0:1, :], surfaces[source, 3:4, :], source
        )
        out[...] = jnp.broadcast_to(edge, out.shape)


def edge_row(left, right):
    lane = lane_ids(left.shape)
    value = jnp.where(lane < HALO, right, 0.0)
    return jnp.where(lane >= LANES - HALO, pltpu.roll(left, LANES - 2 * HALO, 1), value)


def edge_block(left, right):
    gap = jnp.zeros((LANES - 2 * HALO, left.shape[1]), f32)
    return jnp.concatenate([right, gap, left], axis=0).T


def advance(field, rates, constant, left, alive):
    width = field.shape[1]
    live = alive[...] > 0.0
    for _ in range(SUBS):
        near = pltpu.roll(field, 1, 1) + pltpu.roll(field, width - 1, 1)
        spread = field + rates * (near - 2.0 * field)
        stepped = matmul(left, right_operand(spread)) + constant
        field = jnp.where(live, stepped, field)
    return field


def forcing(response, boundary, edge, tendency):
    row = jnp.concatenate([boundary[...], edge], axis=1)
    width = row.shape[1]
    parts = [
        response * row[:, j * LANES : (j + 1) * LANES] for j in range(width // LANES)
    ]
    return jnp.concatenate(parts, axis=1) + tendency


def one_hot(listed, columns):
    row = jnp.concatenate([listed[m : m + 1, :] for m in range(listed.shape[0])], axis=1)
    column = lax.broadcasted_iota(jnp.int32, (columns, row.shape[1]), 0)
    return jnp.where(column == row, 1.0, 0.0).astype(bf16)


def chosen(field, hits):
    levels = field.shape[0]
    high, low = halves(field[:, : hits.shape[0]])
    both = matmul(jnp.concatenate([high, low], axis=0), hits[...])
    both = both[:levels] + both[levels:]
    tiles = hits.shape[1] // 4
    return [both[:, m * tiles : (m + 1) * tiles].T for m in range(4)]


def step_first(
    state, tendency, diffusion, left, response, alive, hits, boundary, odd, even,
    window, rates_out, forcing_out, surface, parcel,
):
    rates = jnp.concatenate(
        [diffusion[...].astype(f32), edge_block(*sides(odd, even, 8, 8))], axis=1
    )
    tend = jnp.concatenate(
        [tendency[...].astype(f32), edge_block(*sides(odd, even, 16, 8))], axis=1
    )
    field = jnp.concatenate([state[...], edge_block(*sides(odd, even, 0, 8))], axis=1)
    edge = edge_row(*sides(odd, even, 24, 1))
    constant = forcing(response[...], boundary, edge, tend)
    rates_out[...] = rates
    forcing_out[...] = tend
    field = advance(field, rates, constant, left[...], alive)
    window[...] = field
    levels = field.shape[0]
    for j in range(4):
        surface[j : j + 1, :] = field[levels - 1 : levels, j * LANES : (j + 1) * LANES]
    for m, rows in enumerate(chosen(field, hits)):
        parcel[m] = rows


def step_second(
    window, rates, tend, left, response, alive, hits, boundary, odd, even, earlier,
    final, parcels,
):
    edge = edge_row(*sides(odd, even, 0, 1))
    constant = forcing(response[...], boundary, edge, tend[...])
    field = advance(window[...], rates[...], constant, left[...], alive)
    final[...] = field[:, : final.shape[1]]
    slots = earlier.shape[0]
    tiles = earlier.shape[1]
    for m in range(slots):
        parcels[pl.ds(m, tiles, stride=2 * slots), :] = earlier[m]
    for m, rows in enumerate(chosen(field, hits)):
        parcels[pl.ds(slots + m, tiles, stride=2 * slots), :] = rows


def ready_first(active, mixing, coupling, listed, left, response, alive, hits):
    width = alive.shape[1]
    lane = lane_ids((1, width))
    column = jnp.where(lane < width - LANES, lane, lane - (width - LANES))
    column = jnp.where(lane < width - HALO, column, lane - LANES)
    alive[...] = jnp.where(column < active[lax.axis_index("sec")], 1.0, 0.0)
    left[...] = left_operand(mixing[...])
    response[...] = jnp.broadcast_to(coupling[...], (LANES, coupling.shape[1])).T
    hits[...] = one_hot(listed[0], hits.shape[0])


def ready_second(listed, slots, weights, counts, refraction, abel, hits, spread, right, right_abel):
    hits[...] = one_hot(listed[1], hits.shape[0])
    right[...] = right_operand(refraction[...])
    right_abel[...] = right_operand(abel[...])
    steps, ranks, occultations = slots.shape
    width = spread.shape[2] // 3
    tiles = width // 4
    for p in range(steps):
        rank = lax.broadcasted_iota(jnp.int32, (ranks, occultations), 0)
        live = jnp.where(rank < counts[p : p + 1, :], weights[p], 0.0).T
        key = ((slots[p] & 3) * tiles + (slots[p] >> 2)).T
        place = lane_ids((occultations, width))
        total = jnp.zeros((occultations, width), f32)
        for k in range(ranks):
            total = total + jnp.where(key[:, k : k + 1] == place, live[:, k : k + 1], 0.0)
        spread[p] = left_operand(total)


def project(arrived, spread, refraction, out):
    steps, occultations, width = spread.shape
    tiles = width // 12
    owners = out.shape[0]
    rows = occultations // owners
    profiles = []
    for p in range(steps):
        values = jnp.concatenate(
            [arrived[pl.ds(4 * p + m, tiles, stride=4 * steps), :] for m in range(4)], axis=0
        )
        profiles.append(matmul(spread[p], right_operand(values)))
    profile = jnp.concatenate(profiles, axis=0)
    projected = matmul(left_operand(profile), refraction[...])
    for p in range(steps):
        for q in range(owners):
            start = p * occultations + q * rows
            out[q, p * rows : (p + 1) * rows, :] = projected[start : start + rows, :]


def depart(received, abel, observed, out):
    total = received[0]
    for s in range(1, received.shape[0]):
        total = total + received[s]
    bending = matmul(left_operand(total), abel[...])
    steps, rows, _ = observed.shape
    for p in range(steps):
        out[p] = observed[p] - bending[p * rows : (p + 1) * rows, :]


def shards(
    state,
    tendency,
    diffusion,
    mixing,
    coupling,
    remap_index,
    remap_weight,
    active_cols,
    send_cols,
    occ_slot,
    occ_weight,
    occ_count,
    refraction,
    abel_matrix,
    observed,
):
    sections = lax.axis_size("sec")
    tiles = lax.axis_size("tile")
    levels, columns = state.shape[1:]
    rows, heights = observed.shape[1:]
    width = columns + LANES
    half = sections // 2
    swaps = ([], [])
    for s in range(sections):
        for t in range(tiles):
            target = ((s + half) % sections if t == tiles - 1 else s) * tiles + (t + 1) % tiles
            swaps[t % 2].extend([(s * tiles + t, target), (target, s * tiles + t)])
    above_even, above_odd = swaps
    listed = jnp.transpose(send_cols[:, 0, 0], (0, 2, 1))
    index, weight = remap_index[0], remap_weight[0]
    shape = jax.ShapeDtypeStruct
    after = lax.optimization_barrier

    edges = call(
        prepare,
        shape((64, LANES), f32),
        *(
            pltpu.with_memory_space_constraint(x, pltpu.HBM)
            for x in (state[0], tendency[0], diffusion[0], index, weight)
        ),
        space=pltpu.HBM,
        scratch=[pltpu.VMEM((levels, LANES), f32)] * 2
        + [pltpu.VMEM((levels, LANES), bf16)] * 4
        + [
            pltpu.VMEM((8, columns), f32),
            pltpu.VMEM(index.shape, jnp.int32),
            pltpu.VMEM(weight.shape, f32),
            pltpu.SemaphoreType.DMA((9,)),
        ],
    )
    shared = lax.all_gather(edges, "sec", axis=0, tiled=False)
    boundary, odd, even = call(
        couple_first,
        (shape((1, columns), f32), shape((32, LANES), f32), shape((32, LANES), f32)),
        shared, index, weight,
    )
    odd = lax.ppermute(odd, AXES, above_odd)
    even = lax.ppermute(even, AXES, above_even)
    mixing_row, _ = after((mixing[0], boundary))
    left, response, alive, hits = call(
        ready_first,
        (
            shape((levels, 3 * levels), bf16),
            shape((levels, LANES), f32),
            shape((1, width), f32),
            shape((columns, 4 * tiles), bf16),
        ),
        active_cols, mixing_row, coupling, listed,
    )
    window, rates, tend, surface, parcel = call(
        step_first,
        (
            shape((levels, width), f32),
            shape((levels, width), f32),
            shape((levels, width), f32),
            shape((4, LANES), f32),
            shape((4, tiles, levels), f32),
        ),
        state[0], tendency[0], diffusion[0], left, response, alive, hits, boundary, odd, even,
    )
    surfaces = lax.all_gather(surface, "sec", axis=0, tiled=False)
    boundary, odd, even = call(
        couple_second,
        (shape((1, columns), f32), shape((8, LANES), f32), shape((8, LANES), f32)),
        surfaces, shared, index, weight,
    )
    odd = lax.ppermute(odd, AXES, above_odd)
    even = lax.ppermute(even, AXES, above_even)
    weights, _ = after((occ_weight[:, 0], boundary))
    hits, spread, right, right_abel = call(
        ready_second,
        (
            shape((columns, 4 * tiles), bf16),
            shape((STEPS, occ_slot.shape[3], 12 * tiles), bf16),
            shape((3 * levels, levels), bf16),
            shape((3 * levels, heights), bf16),
        ),
        listed, occ_slot[:, 0], weights, occ_count[:, 0], refraction[0], abel_matrix,
    )
    final, parcels = call(
        step_second,
        (shape((levels, columns), f32), shape((8 * tiles, levels), f32)),
        window, rates, tend, left, response, alive, hits, boundary, odd, even, parcel,
    )
    parcels, spread, right, right_abel = after((parcels, spread, right, right_abel))
    arrived = lax.all_to_all(
        parcels.reshape(tiles, 8, levels), "tile", split_axis=0, concat_axis=0, tiled=True
    )
    partial = call(
        project,
        shape((sections, STEPS * rows, levels), f32),
        arrived.reshape(8 * tiles, levels), spread, right,
    )
    received = lax.all_to_all(partial, "sec", split_axis=0, concat_axis=0, tiled=True)
    departures = call(
        depart, shape((STEPS, rows, heights), f32), received, right_abel, observed
    )
    return (final[None], departures)


def solution(mesh):
    return jax.shard_map(
        shards,
        mesh=mesh,
        in_specs=(
            P("sec", None, "tile"),
            P("sec", None, "tile"),
            P("sec", None, "tile"),
            P("sec", None, None),
            P("sec", None),
            P("sec", None, "tile"),
            P("sec", None, "tile"),
            P(),
            P(None, "sec", "tile", None, None),
            P(None, "sec", None, "tile"),
            P(None, "sec", None, "tile"),
            P(None, "sec", "tile"),
            P("sec", None, None),
            P(),
            P(None, ("sec", "tile"), None),
        ),
        out_specs=(P("sec", None, "tile"), P(None, ("sec", "tile"), None)),
        check_vma=False,
    )
```

```python
import jax
import jax.numpy as jnp
from jax import lax
from jax.experimental import pallas as pl
from jax.experimental.pallas import tpu as pltpu
from jax.sharding import PartitionSpec as P

SUBS = 4
STEPS = 2
PARTS = 2
HALO = 8
LANES = 128
AXES = ("sec", "tile")
f32 = jnp.float32
bf16 = jnp.bfloat16


def call(body, outs, *args, scratch=(), space=pltpu.VMEM):
    in_specs = [
        pl.BlockSpec(memory_space=pltpu.SMEM if a.ndim == 1 else space) for a in args
    ]
    single = not isinstance(outs, (tuple, list))
    specs = pl.BlockSpec(memory_space=pltpu.VMEM)
    return pl.pallas_call(
        body,
        out_shape=outs if single else tuple(outs),
        in_specs=in_specs,
        out_specs=specs if single else tuple(specs for _ in outs),
        scratch_shapes=list(scratch),
        compiler_params=pltpu.CompilerParams(vmem_limit_bytes=40 * 2**20),
    )(*args)


def halves(x):
    high = x.astype(bf16)
    return high, (x - high.astype(f32)).astype(bf16)


def left_operand(x):
    high, low = halves(x)
    return jnp.concatenate([high, high, low], axis=1)


def right_operand(x):
    high, low = halves(x)
    return jnp.concatenate([high, low, high], axis=0)


def matmul(left, right):
    return jnp.dot(left, right, preferred_element_type=f32)


def pick(table, position):
    lane = position & (LANES - 1)
    row = position >> 7
    out = jnp.zeros(position.shape, f32)
    for r, values in enumerate(table):
        source = jnp.broadcast_to(values, position.shape)
        found = jnp.take_along_axis(source, lane, axis=1, mode="promise_in_bounds")
        out = jnp.where(row == r, found, out)
    return out


def position_offset(columns):
    ocean = lax.axis_size("sec") - 1
    return jnp.where(lax.axis_index("sec") == ocean, 0, ocean * columns)


def edge_sources():
    section, tile = lax.axis_index("sec"), lax.axis_index("tile")
    sections = lax.axis_size("sec")
    other = section + sections // 2
    other = jnp.where(other >= sections, other - sections, other)
    last = lax.axis_size("tile") - 1
    return jnp.where(tile == last, other, section), jnp.where(tile == 0, other, section)


def even_tile():
    return lax.rem(lax.axis_index("tile"), 2) == 0


def sent_edges():
    up, down = edge_sources()
    even = even_tile()
    return (
        (jnp.where(even, down, up), jnp.where(even, 0, HALO)),
        (jnp.where(even, up, down), jnp.where(even, HALO, 0)),
    )


def sides(odd, even, start, rows):
    first, second = odd[start : start + rows, :], even[start : start + rows, :]
    here = even_tile()
    return jnp.where(here, first, second), jnp.where(here, second, first)


def lane_ids(shape):
    return lax.broadcasted_iota(jnp.int32, shape, len(shape) - 1)


def pack_edges(first, last):
    lane = lane_ids(first.shape)
    return jnp.where(lane < HALO, first, pltpu.roll(last, 2 * HALO, 1))


def prepare(state, tendency, diffusion, index, weight, out, *scratch):
    levels, columns = state.shape
    tail = columns - LANES
    *ends, bottom, indices, weights, sems = scratch
    pairs = []
    for ref, head, back in zip((state, diffusion, tendency), ends[::2], ends[1::2]):
        pairs.append((ref.at[:, pl.ds(0, LANES)], head))
        pairs.append((ref.at[:, pl.ds(tail, LANES)], back))
    pairs.append((state.at[pl.ds(levels - 8, 8), :], bottom))
    pairs.append((index, indices))
    pairs.append((weight, weights))
    copies = [
        pltpu.make_async_copy(source, target, sems.at[i])
        for i, (source, target) in enumerate(pairs)
    ]
    for copy in copies:
        copy.start()
    for copy in copies:
        copy.wait()
    block = jnp.zeros((levels, LANES), f32)
    lane = lane_ids(block.shape)
    for i in range(3):
        edges = pack_edges(ends[2 * i][...].astype(f32), ends[2 * i + 1][...].astype(f32))
        if i:
            edges = pltpu.roll(edges, 2 * HALO * i, 1)
        inside = (lane >= 2 * HALO * i) & (lane < 2 * HALO * (i + 1))
        block = jnp.where(inside, edges, block)
    out[0:48, :] = block.T[0:48, :]
    for j in range(columns // LANES):
        out[48 + j : 49 + j, :] = bottom[7:8, j * LANES : (j + 1) * LANES]
    out[52:56, :] = pack_edges(weights[:, :LANES], weights[:, tail:])
    position = (indices[...] + position_offset(columns)).astype(f32)
    out[56:60, :] = pack_edges(position[:, :LANES], position[:, tail:])
    out[60:64, :] = jnp.zeros((4, LANES), f32)


def edge_boundary(table, shared, surface_first, surface_last, source):
    position = shared[source, 56:60, :].astype(jnp.int32)
    picked = pick(table, position)
    partner = jnp.sum(shared[source, 52:56, :] * picked, axis=0, keepdims=True)
    return partner - pack_edges(surface_first, surface_last)


def own_boundary(table, index, weight, surface, out):
    offset = position_offset(out.shape[1])
    for j in range(out.shape[1] // LANES):
        cut = slice(j * LANES, (j + 1) * LANES)
        picked = pick(table, index[:, cut] + offset)
        partner = jnp.sum(weight[:, cut] * picked, axis=0, keepdims=True)
        out[:, cut] = partner - surface(j)


def couple_first(shared, index, weight, boundary, odd, even):
    section = lax.axis_index("sec")
    table = [shared[s, r : r + 1, :] for s in range(shared.shape[0]) for r in range(48, 52)]
    own_boundary(
        table, index, weight, lambda j: shared[section, 48 + j : 49 + j, :], boundary
    )
    for out, (source, start) in zip((odd, even), sent_edges()):
        for i in range(3):
            row = pl.multiple_of(2 * HALO * i + start, HALO)
            out[HALO * i : HALO * (i + 1), :] = shared[source, pl.ds(row, HALO), :]
        edge = edge_boundary(
            table, shared, shared[source, 48:49, :], shared[source, 51:52, :], source
        )
        out[24:32, :] = jnp.broadcast_to(edge, (8, LANES))


def couple_second(surfaces, shared, index, weight, boundary, odd, even):
    section = lax.axis_index("sec")
    table = [surfaces[s, r : r + 1, :] for s in range(surfaces.shape[0]) for r in range(4)]
    own_boundary(
        table, index, weight, lambda j: surfaces[section, j : j + 1, :], boundary
    )
    for out, (source, _) in zip((odd, even), sent_edges()):
        edge = edge_boundary(
            table, shared, surfaces[source, 0:1, :], surfaces[source, 3:4, :], source
        )
        out[...] = jnp.broadcast_to(edge, out.shape)


def edge_row(left, right):
    lane = lane_ids(left.shape)
    value = jnp.where(lane < HALO, right, 0.0)
    return jnp.where(lane >= LANES - HALO, pltpu.roll(left, LANES - 2 * HALO, 1), value)


def edge_block(left, right):
    gap = jnp.zeros((LANES - 2 * HALO, left.shape[1]), f32)
    return jnp.concatenate([right, gap, left], axis=0).T


def advance(field, rates, constant, left, alive):
    width = field.shape[1]
    live = alive[...] > 0.0
    for _ in range(SUBS):
        near = pltpu.roll(field, 1, 1) + pltpu.roll(field, width - 1, 1)
        spread = field + rates * (near - 2.0 * field)
        stepped = matmul(left, right_operand(spread)) + constant
        field = jnp.where(live, stepped, field)
    return field


def forcing(response, boundary, edge, tendency):
    row = jnp.concatenate([boundary[...], edge], axis=1)
    width = row.shape[1]
    parts = [
        response * row[:, j * LANES : (j + 1) * LANES] for j in range(width // LANES)
    ]
    return jnp.concatenate(parts, axis=1) + tendency


def one_hot(listed, columns):
    row = jnp.concatenate([listed[m : m + 1, :] for m in range(listed.shape[0])], axis=1)
    column = lax.broadcasted_iota(jnp.int32, (columns, row.shape[1]), 0)
    return jnp.where(column == row, 1.0, 0.0).astype(bf16)


def chosen(field, hits):
    levels = field.shape[0]
    high, low = halves(field[:, : hits.shape[0]])
    both = matmul(jnp.concatenate([high, low], axis=0), hits[...])
    both = both[:levels] + both[levels:]
    tiles = hits.shape[1] // 4
    return [both[:, m * tiles : (m + 1) * tiles].T for m in range(4)]


def step_first(
    state, tendency, diffusion, left, response, alive, hits, boundary, odd, even,
    window, rates_out, forcing_out, surface, parcel,
):
    rates = jnp.concatenate(
        [diffusion[...].astype(f32), edge_block(*sides(odd, even, 8, 8))], axis=1
    )
    tend = jnp.concatenate(
        [tendency[...].astype(f32), edge_block(*sides(odd, even, 16, 8))], axis=1
    )
    field = jnp.concatenate([state[...], edge_block(*sides(odd, even, 0, 8))], axis=1)
    edge = edge_row(*sides(odd, even, 24, 1))
    constant = forcing(response[...], boundary, edge, tend)
    rates_out[...] = rates
    forcing_out[...] = tend
    field = advance(field, rates, constant, left[...], alive)
    window[...] = field
    levels = field.shape[0]
    for j in range(4):
        surface[j : j + 1, :] = field[levels - 1 : levels, j * LANES : (j + 1) * LANES]
    for m, rows in enumerate(chosen(field, hits)):
        parcel[m] = rows


def step_second(
    window, rates, tend, left, response, alive, hits, boundary, odd, even, earlier,
    final, parcels,
):
    edge = edge_row(*sides(odd, even, 0, 1))
    constant = forcing(response[...], boundary, edge, tend[...])
    field = advance(window[...], rates[...], constant, left[...], alive)
    final[...] = field[:, : final.shape[1]]
    slots, tiles, _ = earlier.shape
    part = tiles // PARTS
    width = PARTS * STEPS * slots
    for m, later in enumerate(chosen(field, hits)):
        for o in range(PARTS):
            for p, rows in enumerate((earlier[m], later)):
                first = (o * STEPS + p) * slots + m
                owned = rows[o * part : (o + 1) * part]
                parcels[pl.ds(first, part, stride=width), :] = owned


def ready_first(
    active, mixing, coupling, listed, slots, weights, counts, left, response, alive, hits, lists
):
    steps, ranks, occultations = slots.shape
    for p in range(steps):
        rank = lax.broadcasted_iota(jnp.int32, (ranks, occultations), 0)
        lists[p * ranks : (p + 1) * ranks, :] = slots[p].astype(f32)
        live = jnp.where(rank < counts[p : p + 1, :], weights[p], 0.0)
        lists[(steps + p) * ranks : (steps + p + 1) * ranks, :] = live
    width = alive.shape[1]
    lane = lane_ids((1, width))
    column = jnp.where(lane < width - LANES, lane, lane - (width - LANES))
    column = jnp.where(lane < width - HALO, column, lane - LANES)
    alive[...] = jnp.where(column < active[lax.axis_index("sec")], 1.0, 0.0)
    left[...] = left_operand(mixing[...])
    response[...] = jnp.broadcast_to(coupling[...], (LANES, coupling.shape[1])).T
    hits[...] = one_hot(listed[0], hits.shape[0])


def ready_second(listed, lists, mirrored, refraction, abel, hits, spread, right, right_abel):
    hits[...] = one_hot(listed[1], hits.shape[0])
    right[...] = right_operand(refraction[...])
    right_abel[...] = right_operand(abel[...])
    occultations, width = spread.shape[2], spread.shape[3] // 3
    ranks = lists.shape[0] // (2 * STEPS)
    part = width // 4
    here = jnp.where(lax.axis_index("tile") >= part, 1, 0)
    place = lane_ids((occultations, width))
    for o in range(PARTS):
        owned = jnp.where(here == o, lists[...], mirrored[...])
        for p in range(STEPS):
            slot = owned[p * ranks : (p + 1) * ranks].astype(jnp.int32)
            live = owned[(STEPS + p) * ranks : (STEPS + p + 1) * ranks].T
            source = (slot >> 2) - here * part
            inside = (source >= 0) & (source < part)
            key = jnp.where(inside, (slot & 3) * part + source, -1).T
            total = jnp.zeros((occultations, width), f32)
            for k in range(ranks):
                hit = key[:, k : k + 1] == place
                total = total + jnp.where(hit, live[:, k : k + 1], 0.0)
            spread[o, p] = left_operand(total)


def project(arrived, spread, refraction, kept, sent):
    occultations, width = spread.shape[2:]
    part = width // 12
    profiles = []
    for o in range(PARTS):
        for p in range(STEPS):
            first = 4 * (o * STEPS + p)
            values = jnp.concatenate(
                [
                    arrived[pl.ds(first + m, part, stride=4 * PARTS * STEPS), :]
                    for m in range(4)
                ],
                axis=0,
            )
            profiles.append(matmul(spread[o, p], right_operand(values)))
    profile = jnp.concatenate(profiles, axis=0)
    projected = matmul(left_operand(profile), refraction[...])
    pairs = kept.shape[0] // PARTS
    rows = occultations // (2 * pairs)
    first_core = lax.rem(lax.axis_index("sec"), 2) == 0
    for o in range(PARTS):
        for p in range(STEPS):
            for pair in range(pairs):
                start = (o * STEPS + p) * occultations + 2 * pair * rows
                low = projected[start : start + rows]
                high = projected[start + rows : start + 2 * rows]
                target = (pair * PARTS + o, slice(p * rows, (p + 1) * rows))
                kept[target] = jnp.where(first_core, low, high)
                sent[target] = jnp.where(first_core, high, low)


def depart(received, abel, observed, out):
    total = received[0]
    for s in range(1, received.shape[0]):
        total = total + received[s]
    bending = matmul(left_operand(total), abel[...])
    steps, rows, _ = observed.shape
    for p in range(steps):
        out[p] = observed[p] - bending[p * rows : (p + 1) * rows, :]


def shards(
    state,
    tendency,
    diffusion,
    mixing,
    coupling,
    remap_index,
    remap_weight,
    active_cols,
    send_cols,
    occ_slot,
    occ_weight,
    occ_count,
    refraction,
    abel_matrix,
    observed,
):
    sections = lax.axis_size("sec")
    tiles = lax.axis_size("tile")
    levels, columns = state.shape[1:]
    rows, heights = observed.shape[1:]
    width = columns + LANES
    half = sections // 2
    part = tiles // PARTS
    ranks, owned = occ_slot.shape[2:]
    swaps = ([], [])
    for s in range(sections):
        for t in range(tiles):
            target = ((s + half) % sections if t == tiles - 1 else s) * tiles + (t + 1) % tiles
            swaps[t % 2].extend([(s * tiles + t, target), (target, s * tiles + t)])
    above_even, above_odd = swaps
    listed = jnp.transpose(send_cols[:, 0, 0], (0, 2, 1))
    index, weight = remap_index[0], remap_weight[0]
    shape = jax.ShapeDtypeStruct
    after = lax.optimization_barrier

    edges = call(
        prepare,
        shape((64, LANES), f32),
        *(
            pltpu.with_memory_space_constraint(x, pltpu.HBM)
            for x in (state[0], tendency[0], diffusion[0], index, weight)
        ),
        space=pltpu.HBM,
        scratch=[pltpu.VMEM((levels, LANES), f32)] * 2
        + [pltpu.VMEM((levels, LANES), bf16)] * 4
        + [
            pltpu.VMEM((8, columns), f32),
            pltpu.VMEM(index.shape, jnp.int32),
            pltpu.VMEM(weight.shape, f32),
            pltpu.SemaphoreType.DMA((9,)),
        ],
    )
    shared = lax.all_gather(edges, "sec", axis=0, tiled=False)
    boundary, odd, even = call(
        couple_first,
        (shape((1, columns), f32), shape((32, LANES), f32), shape((32, LANES), f32)),
        shared, index, weight,
    )
    odd = lax.ppermute(odd, AXES, above_odd)
    even = lax.ppermute(even, AXES, above_even)
    mixing_row, _ = after((mixing[0], boundary))
    left, response, alive, hits, lists = call(
        ready_first,
        (
            shape((levels, 3 * levels), bf16),
            shape((levels, LANES), f32),
            shape((1, width), f32),
            shape((columns, 4 * tiles), bf16),
            shape((2 * STEPS * ranks, owned), f32),
        ),
        active_cols, mixing_row, coupling, listed, occ_slot[:, 0], occ_weight[:, 0], occ_count[:, 0],
    )
    mirrored = lax.ppermute(
        lists, "tile", [(t, (t + part) % tiles) for t in range(tiles)]
    )
    window, rates, tend, surface, parcel = call(
        step_first,
        (
            shape((levels, width), f32),
            shape((levels, width), f32),
            shape((levels, width), f32),
            shape((4, LANES), f32),
            shape((4, tiles, levels), f32),
        ),
        state[0], tendency[0], diffusion[0], left, response, alive, hits, boundary, odd, even,
    )
    surfaces = lax.all_gather(surface, "sec", axis=0, tiled=False)
    boundary, odd, even = call(
        couple_second,
        (shape((1, columns), f32), shape((8, LANES), f32), shape((8, LANES), f32)),
        surfaces, shared, index, weight,
    )
    odd = lax.ppermute(odd, AXES, above_odd)
    even = lax.ppermute(even, AXES, above_even)
    mirrored, _ = after((mirrored, boundary))
    hits, spread, right, right_abel = call(
        ready_second,
        (
            shape((columns, 4 * tiles), bf16),
            shape((PARTS, STEPS, owned, 12 * part), bf16),
            shape((3 * levels, levels), bf16),
            shape((3 * levels, heights), bf16),
        ),
        listed, lists, mirrored, refraction[0], abel_matrix,
    )
    final, parcels = call(
        step_second,
        (shape((levels, columns), f32), shape((8 * tiles, levels), f32)),
        window, rates, tend, left, response, alive, hits, boundary, odd, even, parcel,
    )
    parcels, spread, right, right_abel = after((parcels, spread, right, right_abel))
    arrived = lax.all_to_all(
        parcels.reshape(part, 8 * PARTS, levels),
        "tile",
        split_axis=0,
        concat_axis=0,
        axis_index_groups=[[o * part + i for i in range(part)] for o in range(PARTS)],
        tiled=True,
    )
    block = shape((half * PARTS, STEPS * rows, levels), f32)
    kept, sent = call(
        project, (block, block), arrived.reshape(8 * PARTS * part, levels), spread, right
    )
    got = lax.ppermute(sent, "sec", [(s, s ^ 1) for s in range(sections)])
    received = lax.all_to_all(
        kept + got,
        AXES,
        split_axis=0,
        concat_axis=0,
        axis_index_groups=[
            [(2 * z + core) * tiles + o * part + i for z in range(half) for o in range(PARTS)]
            for core in range(2)
            for i in range(part)
        ],
        tiled=True,
    )
    departures = call(
        depart, shape((STEPS, rows, heights), f32), received, right_abel, observed
    )
    return (final[None], departures)


def solution(mesh):
    return jax.shard_map(
        shards,
        mesh=mesh,
        in_specs=(
            P("sec", None, "tile"),
            P("sec", None, "tile"),
            P("sec", None, "tile"),
            P("sec", None, None),
            P("sec", None),
            P("sec", None, "tile"),
            P("sec", None, "tile"),
            P(),
            P(None, "sec", "tile", None, None),
            P(None, "sec", None, "tile"),
            P(None, "sec", None, "tile"),
            P(None, "sec", "tile"),
            P("sec", None, None),
            P(),
            P(None, ("sec", "tile"), None),
        ),
        out_specs=(P("sec", None, "tile"), P(None, ("sec", "tile"), None)),
        check_vma=False,
    )
```

```python
import jax
import jax.numpy as jnp
from jax import lax
from jax.experimental import pallas as pl
from jax.experimental.pallas import tpu as pltpu
from jax.sharding import PartitionSpec as P

SUBS = 4
STEPS = 2
PARTS = 2
HALO = 8
LANES = 128
AXES = ("sec", "tile")
f32 = jnp.float32
bf16 = jnp.bfloat16


def call(body, outs, *args, scratch=(), space=pltpu.VMEM):
    in_specs = [
        pl.BlockSpec(memory_space=pltpu.SMEM if a.ndim == 1 else space) for a in args
    ]
    single = not isinstance(outs, (tuple, list))
    specs = pl.BlockSpec(memory_space=pltpu.VMEM)
    return pl.pallas_call(
        body,
        out_shape=outs if single else tuple(outs),
        in_specs=in_specs,
        out_specs=specs if single else tuple(specs for _ in outs),
        scratch_shapes=list(scratch),
        compiler_params=pltpu.CompilerParams(vmem_limit_bytes=40 * 2**20),
    )(*args)


def halves(x):
    high = x.astype(bf16)
    return high, (x - high.astype(f32)).astype(bf16)


def left_operand(x):
    high, low = halves(x)
    return jnp.concatenate([high, high, low], axis=1)


def right_operand(x):
    high, low = halves(x)
    return jnp.concatenate([high, low, high], axis=0)


def matmul(left, right):
    return jnp.dot(left, right, preferred_element_type=f32)


def pick(table, position):
    lane = position & (LANES - 1)
    row = position >> 7
    out = jnp.zeros(position.shape, f32)
    for r, values in enumerate(table):
        source = jnp.broadcast_to(values, position.shape)
        found = jnp.take_along_axis(source, lane, axis=1, mode="promise_in_bounds")
        out = jnp.where(row == r, found, out)
    return out


def position_offset(columns):
    ocean = lax.axis_size("sec") - 1
    return jnp.where(lax.axis_index("sec") == ocean, 0, ocean * columns)


def edge_sources():
    section, tile = lax.axis_index("sec"), lax.axis_index("tile")
    sections = lax.axis_size("sec")
    other = section + sections // 2
    other = jnp.where(other >= sections, other - sections, other)
    last = lax.axis_size("tile") - 1
    return jnp.where(tile == last, other, section), jnp.where(tile == 0, other, section)


def even_tile():
    return lax.rem(lax.axis_index("tile"), 2) == 0


def sent_edges():
    up, down = edge_sources()
    even = even_tile()
    return (
        (jnp.where(even, down, up), jnp.where(even, 0, HALO)),
        (jnp.where(even, up, down), jnp.where(even, HALO, 0)),
    )


def sides(odd, even, start, rows):
    first, second = odd[start : start + rows, :], even[start : start + rows, :]
    here = even_tile()
    return jnp.where(here, first, second), jnp.where(here, second, first)


def lane_ids(shape):
    return lax.broadcasted_iota(jnp.int32, shape, len(shape) - 1)


def pack_edges(first, last):
    lane = lane_ids(first.shape)
    return jnp.where(lane < HALO, first, pltpu.roll(last, 2 * HALO, 1))


def prepare(state, tendency, diffusion, index, weight, out, *scratch):
    levels, columns = state.shape
    tail = columns - LANES
    *ends, bottom, indices, weights, sems = scratch
    pairs = []
    for ref, head, back in zip((state, diffusion, tendency), ends[::2], ends[1::2]):
        pairs.append((ref.at[:, pl.ds(0, LANES)], head))
        pairs.append((ref.at[:, pl.ds(tail, LANES)], back))
    pairs.append((state.at[pl.ds(levels - 8, 8), :], bottom))
    pairs.append((index, indices))
    pairs.append((weight, weights))
    copies = [
        pltpu.make_async_copy(source, target, sems.at[i])
        for i, (source, target) in enumerate(pairs)
    ]
    for copy in copies:
        copy.start()
    for copy in copies:
        copy.wait()
    block = jnp.zeros((levels, LANES), f32)
    lane = lane_ids(block.shape)
    for i in range(3):
        edges = pack_edges(ends[2 * i][...].astype(f32), ends[2 * i + 1][...].astype(f32))
        if i:
            edges = pltpu.roll(edges, 2 * HALO * i, 1)
        inside = (lane >= 2 * HALO * i) & (lane < 2 * HALO * (i + 1))
        block = jnp.where(inside, edges, block)
    out[0:48, :] = block.T[0:48, :]
    for j in range(columns // LANES):
        out[48 + j : 49 + j, :] = bottom[7:8, j * LANES : (j + 1) * LANES]
    out[52:56, :] = pack_edges(weights[:, :LANES], weights[:, tail:])
    position = (indices[...] + position_offset(columns)).astype(f32)
    out[56:60, :] = pack_edges(position[:, :LANES], position[:, tail:])
    out[60:64, :] = jnp.zeros((4, LANES), f32)


def edge_boundary(table, shared, surface_first, surface_last, source):
    position = shared[source, 56:60, :].astype(jnp.int32)
    picked = pick(table, position)
    partner = jnp.sum(shared[source, 52:56, :] * picked, axis=0, keepdims=True)
    return partner - pack_edges(surface_first, surface_last)


def own_boundary(table, index, weight, surface, out):
    offset = position_offset(out.shape[1])
    for j in range(out.shape[1] // LANES):
        cut = slice(j * LANES, (j + 1) * LANES)
        picked = pick(table, index[:, cut] + offset)
        partner = jnp.sum(weight[:, cut] * picked, axis=0, keepdims=True)
        out[:, cut] = partner - surface(j)


def couple_first(
    shared, index, weight, slots, weights, counts, boundary, odd, lists, even
):
    steps, ranks, occultations = slots.shape
    for p in range(steps):
        rank = lax.broadcasted_iota(jnp.int32, (ranks, occultations), 0)
        lists[p * ranks : (p + 1) * ranks, :] = slots[p].astype(f32)
        live = jnp.where(rank < counts[p : p + 1, :], weights[p], 0.0)
        lists[(steps + p) * ranks : (steps + p + 1) * ranks, :] = live
    section = lax.axis_index("sec")
    table = [shared[s, r : r + 1, :] for s in range(shared.shape[0]) for r in range(48, 52)]
    own_boundary(
        table, index, weight, lambda j: shared[section, 48 + j : 49 + j, :], boundary
    )
    for out, (source, start) in zip((odd, even), sent_edges()):
        for i in range(3):
            row = pl.multiple_of(2 * HALO * i + start, HALO)
            out[HALO * i : HALO * (i + 1), :] = shared[source, pl.ds(row, HALO), :]
        edge = edge_boundary(
            table, shared, shared[source, 48:49, :], shared[source, 51:52, :], source
        )
        out[24:32, :] = jnp.broadcast_to(edge, (8, LANES))


def couple_second(surfaces, shared, index, weight, boundary, odd, even):
    section = lax.axis_index("sec")
    table = [surfaces[s, r : r + 1, :] for s in range(surfaces.shape[0]) for r in range(4)]
    own_boundary(
        table, index, weight, lambda j: surfaces[section, j : j + 1, :], boundary
    )
    for out, (source, _) in zip((odd, even), sent_edges()):
        edge = edge_boundary(
            table, shared, surfaces[source, 0:1, :], surfaces[source, 3:4, :], source
        )
        out[...] = jnp.broadcast_to(edge, out.shape)


def edge_row(left, right):
    lane = lane_ids(left.shape)
    value = jnp.where(lane < HALO, right, 0.0)
    return jnp.where(lane >= LANES - HALO, pltpu.roll(left, LANES - 2 * HALO, 1), value)


def edge_block(left, right):
    gap = jnp.zeros((LANES - 2 * HALO, left.shape[1]), f32)
    return jnp.concatenate([right, gap, left], axis=0).T


def advance(field, rates, constant, left, alive):
    width = field.shape[1]
    live = alive[...] > 0.0
    for _ in range(SUBS):
        near = pltpu.roll(field, 1, 1) + pltpu.roll(field, width - 1, 1)
        spread = field + rates * (near - 2.0 * field)
        stepped = matmul(left, right_operand(spread)) + constant
        field = jnp.where(live, stepped, field)
    return field


def forcing(response, boundary, edge, tendency):
    row = jnp.concatenate([boundary[...], edge], axis=1)
    width = row.shape[1]
    parts = [
        response * row[:, j * LANES : (j + 1) * LANES] for j in range(width // LANES)
    ]
    return jnp.concatenate(parts, axis=1) + tendency


def one_hot(listed, columns):
    row = jnp.concatenate([listed[m : m + 1, :] for m in range(listed.shape[0])], axis=1)
    column = lax.broadcasted_iota(jnp.int32, (columns, row.shape[1]), 0)
    return jnp.where(column == row, 1.0, 0.0).astype(bf16)


def chosen(field, hits):
    levels = field.shape[0]
    high, low = halves(field[:, : hits.shape[0]])
    both = matmul(jnp.concatenate([high, low], axis=0), hits[...])
    both = both[:levels] + both[levels:]
    tiles = hits.shape[1] // 4
    return [both[:, m * tiles : (m + 1) * tiles].T for m in range(4)]


def step_first(
    state, tendency, diffusion, left, response, alive, hits, boundary, odd, even,
    window, rates_out, forcing_out, surface, parcel,
):
    rates = jnp.concatenate(
        [diffusion[...].astype(f32), edge_block(*sides(odd, even, 8, 8))], axis=1
    )
    tend = jnp.concatenate(
        [tendency[...].astype(f32), edge_block(*sides(odd, even, 16, 8))], axis=1
    )
    field = jnp.concatenate([state[...], edge_block(*sides(odd, even, 0, 8))], axis=1)
    edge = edge_row(*sides(odd, even, 24, 1))
    constant = forcing(response[...], boundary, edge, tend)
    rates_out[...] = rates
    forcing_out[...] = tend
    field = advance(field, rates, constant, left[...], alive)
    window[...] = field
    levels = field.shape[0]
    for j in range(4):
        surface[j : j + 1, :] = field[levels - 1 : levels, j * LANES : (j + 1) * LANES]
    for m, rows in enumerate(chosen(field, hits)):
        parcel[m] = rows


def step_second(
    window, rates, tend, left, response, alive, hits, boundary, odd, even, earlier,
    final, parcels,
):
    edge = edge_row(*sides(odd, even, 0, 1))
    constant = forcing(response[...], boundary, edge, tend[...])
    field = advance(window[...], rates[...], constant, left[...], alive)
    final[...] = field[:, : final.shape[1]]
    slots, tiles, _ = earlier.shape
    part = tiles // PARTS
    width = PARTS * STEPS * slots
    for m, later in enumerate(chosen(field, hits)):
        for o in range(PARTS):
            for p, rows in enumerate((earlier[m], later)):
                first = (o * STEPS + p) * slots + m
                owned = rows[o * part : (o + 1) * part]
                parcels[pl.ds(first, part, stride=width), :] = owned


def ready_first(active, mixing, coupling, listed, left, response, alive, hits):
    width = alive.shape[1]
    lane = lane_ids((1, width))
    column = jnp.where(lane < width - LANES, lane, lane - (width - LANES))
    column = jnp.where(lane < width - HALO, column, lane - LANES)
    alive[...] = jnp.where(column < active[lax.axis_index("sec")], 1.0, 0.0)
    left[...] = left_operand(mixing[...])
    response[...] = jnp.broadcast_to(coupling[...], (LANES, coupling.shape[1])).T
    hits[...] = one_hot(listed[0], hits.shape[0])


def ready_second(listed, lists, mirrored, refraction, abel, hits, spread, right, right_abel):
    hits[...] = one_hot(listed[1], hits.shape[0])
    right[...] = right_operand(refraction[...])
    right_abel[...] = right_operand(abel[...])
    occultations, width = spread.shape[2], spread.shape[3] // 3
    ranks = lists.shape[0] // (2 * STEPS)
    part = width // 4
    here = jnp.where(lax.axis_index("tile") >= part, 1, 0)
    place = lane_ids((occultations, width))
    for o in range(PARTS):
        owned = jnp.where(here == o, lists[...], mirrored[...])
        for p in range(STEPS):
            slot = owned[p * ranks : (p + 1) * ranks].astype(jnp.int32)
            live = owned[(STEPS + p) * ranks : (STEPS + p + 1) * ranks].T
            source = (slot >> 2) - here * part
            inside = (source >= 0) & (source < part)
            key = jnp.where(inside, (slot & 3) * part + source, -1).T
            total = jnp.zeros((occultations, width), f32)
            for k in range(ranks):
                hit = key[:, k : k + 1] == place
                total = total + jnp.where(hit, live[:, k : k + 1], 0.0)
            spread[o, p] = left_operand(total)


def project(arrived, spread, refraction, kept, sent):
    occultations, width = spread.shape[2:]
    part = width // 12
    profiles = []
    for o in range(PARTS):
        for p in range(STEPS):
            first = 4 * (o * STEPS + p)
            values = jnp.concatenate(
                [
                    arrived[pl.ds(first + m, part, stride=4 * PARTS * STEPS), :]
                    for m in range(4)
                ],
                axis=0,
            )
            profiles.append(matmul(spread[o, p], right_operand(values)))
    profile = jnp.concatenate(profiles, axis=0)
    projected = matmul(left_operand(profile), refraction[...])
    pairs = kept.shape[0] // PARTS
    rows = occultations // (2 * pairs)
    first_core = lax.rem(lax.axis_index("sec"), 2) == 0
    for o in range(PARTS):
        for p in range(STEPS):
            for pair in range(pairs):
                start = (o * STEPS + p) * occultations + 2 * pair * rows
                low = projected[start : start + rows]
                high = projected[start + rows : start + 2 * rows]
                target = (pair * PARTS + o, slice(p * rows, (p + 1) * rows))
                kept[target] = jnp.where(first_core, low, high)
                sent[target] = jnp.where(first_core, high, low)


def depart(received, abel, observed, out):
    total = received[0]
    for s in range(1, received.shape[0]):
        total = total + received[s]
    bending = matmul(left_operand(total), abel[...])
    steps, rows, _ = observed.shape
    for p in range(steps):
        out[p] = observed[p] - bending[p * rows : (p + 1) * rows, :]


def shards(
    state,
    tendency,
    diffusion,
    mixing,
    coupling,
    remap_index,
    remap_weight,
    active_cols,
    send_cols,
    occ_slot,
    occ_weight,
    occ_count,
    refraction,
    abel_matrix,
    observed,
):
    sections = lax.axis_size("sec")
    tiles = lax.axis_size("tile")
    levels, columns = state.shape[1:]
    rows, heights = observed.shape[1:]
    width = columns + LANES
    half = sections // 2
    part = tiles // PARTS
    ranks, owned = occ_slot.shape[2:]
    swaps = ([], [])
    for s in range(sections):
        for t in range(tiles):
            target = ((s + half) % sections if t == tiles - 1 else s) * tiles + (t + 1) % tiles
            swaps[t % 2].extend([(s * tiles + t, target), (target, s * tiles + t)])
    above_even, above_odd = swaps
    listed = jnp.transpose(send_cols[:, 0, 0], (0, 2, 1))
    index, weight = remap_index[0], remap_weight[0]
    shape = jax.ShapeDtypeStruct
    after = lax.optimization_barrier

    edges = call(
        prepare,
        shape((64, LANES), f32),
        *(
            pltpu.with_memory_space_constraint(x, pltpu.HBM)
            for x in (state[0], tendency[0], diffusion[0], index, weight)
        ),
        space=pltpu.HBM,
        scratch=[pltpu.VMEM((levels, LANES), f32)] * 2
        + [pltpu.VMEM((levels, LANES), bf16)] * 4
        + [
            pltpu.VMEM((8, columns), f32),
            pltpu.VMEM(index.shape, jnp.int32),
            pltpu.VMEM(weight.shape, f32),
            pltpu.SemaphoreType.DMA((9,)),
        ],
    )
    shared = lax.all_gather(edges, "sec", axis=0, tiled=False)
    boundary, odd, lists, even = call(
        couple_first,
        (
            shape((1, columns), f32),
            shape((32, LANES), f32),
            shape((2 * STEPS * ranks, owned), f32),
            shape((32, LANES), f32),
        ),
        shared, index, weight, occ_slot[:, 0], occ_weight[:, 0], occ_count[:, 0],
    )
    odd = lax.ppermute(odd, AXES, above_odd)
    mirrored = lax.ppermute(lists, "tile", [(t, (t + part) % tiles) for t in range(tiles)])
    even = lax.ppermute(even, AXES, above_even)
    mixing_row, _ = after((mixing[0], boundary))
    left, response, alive, hits = call(
        ready_first,
        (
            shape((levels, 3 * levels), bf16),
            shape((levels, LANES), f32),
            shape((1, width), f32),
            shape((columns, 4 * tiles), bf16),
        ),
        active_cols, mixing_row, coupling, listed,
    )
    window, rates, tend, surface, parcel = call(
        step_first,
        (
            shape((levels, width), f32),
            shape((levels, width), f32),
            shape((levels, width), f32),
            shape((4, LANES), f32),
            shape((4, tiles, levels), f32),
        ),
        state[0], tendency[0], diffusion[0], left, response, alive, hits, boundary, odd, even,
    )
    surfaces = lax.all_gather(surface, "sec", axis=0, tiled=False)
    boundary, odd, even = call(
        couple_second,
        (shape((1, columns), f32), shape((8, LANES), f32), shape((8, LANES), f32)),
        surfaces, shared, index, weight,
    )
    odd = lax.ppermute(odd, AXES, above_odd)
    even = lax.ppermute(even, AXES, above_even)
    mirrored, _ = after((mirrored, boundary))
    hits, spread, right, right_abel = call(
        ready_second,
        (
            shape((columns, 4 * tiles), bf16),
            shape((PARTS, STEPS, owned, 12 * part), bf16),
            shape((3 * levels, levels), bf16),
            shape((3 * levels, heights), bf16),
        ),
        listed, lists, mirrored, refraction[0], abel_matrix,
    )
    final, parcels = call(
        step_second,
        (shape((levels, columns), f32), shape((8 * tiles, levels), f32)),
        window, rates, tend, left, response, alive, hits, boundary, odd, even, parcel,
    )
    parcels, spread, right, right_abel = after((parcels, spread, right, right_abel))
    arrived = lax.all_to_all(
        parcels.reshape(part, 8 * PARTS, levels),
        "tile",
        split_axis=0,
        concat_axis=0,
        axis_index_groups=[[o * part + i for i in range(part)] for o in range(PARTS)],
        tiled=True,
    )
    block = shape((half * PARTS, STEPS * rows, levels), f32)
    kept, sent = call(
        project, (block, block), arrived.reshape(8 * PARTS * part, levels), spread, right
    )
    got = lax.ppermute(sent, "sec", [(s, s ^ 1) for s in range(sections)])
    received = lax.all_to_all(
        kept + got,
        AXES,
        split_axis=0,
        concat_axis=0,
        axis_index_groups=[
            [(2 * z + core) * tiles + o * part + i for z in range(half) for o in range(PARTS)]
            for core in range(2)
            for i in range(part)
        ],
        tiled=True,
    )
    departures = call(
        depart, shape((STEPS, rows, heights), f32), received, right_abel, observed
    )
    return (final[None], departures)


def solution(mesh):
    return jax.shard_map(
        shards,
        mesh=mesh,
        in_specs=(
            P("sec", None, "tile"),
            P("sec", None, "tile"),
            P("sec", None, "tile"),
            P("sec", None, None),
            P("sec", None),
            P("sec", None, "tile"),
            P("sec", None, "tile"),
            P(),
            P(None, "sec", "tile", None, None),
            P(None, "sec", None, "tile"),
            P(None, "sec", None, "tile"),
            P(None, "sec", "tile"),
            P("sec", None, None),
            P(),
            P(None, ("sec", "tile"), None),
        ),
        out_specs=(P("sec", None, "tile"), P(None, ("sec", "tile"), None)),
        check_vma=False,
    )
```

```python
import jax
import jax.numpy as jnp
from jax import lax
from jax.experimental import pallas as pl
from jax.experimental.pallas import tpu as pltpu
from jax.sharding import PartitionSpec as P

SUBS = 4
STEPS = 2
PARTS = 2
HALO = 8
LANES = 128
AXES = ("sec", "tile")
f32 = jnp.float32
bf16 = jnp.bfloat16


def call(body, outs, *args, scratch=(), space=pltpu.VMEM):
    in_specs = [
        pl.BlockSpec(memory_space=pltpu.SMEM if a.ndim == 1 else space) for a in args
    ]
    single = not isinstance(outs, (tuple, list))
    specs = pl.BlockSpec(memory_space=pltpu.VMEM)
    return pl.pallas_call(
        body,
        out_shape=outs if single else tuple(outs),
        in_specs=in_specs,
        out_specs=specs if single else tuple(specs for _ in outs),
        scratch_shapes=list(scratch),
        compiler_params=pltpu.CompilerParams(vmem_limit_bytes=40 * 2**20),
    )(*args)


def halves(x):
    high = x.astype(bf16)
    return high, (x - high.astype(f32)).astype(bf16)


def left_operand(x):
    high, low = halves(x)
    return jnp.concatenate([high, high, low], axis=1)


def right_operand(x):
    high, low = halves(x)
    return jnp.concatenate([high, low, high], axis=0)


def matmul(left, right):
    return jnp.dot(left, right, preferred_element_type=f32)


def pick(table, position):
    lane = position & (LANES - 1)
    row = position >> 7
    out = jnp.zeros(position.shape, f32)
    for r, values in enumerate(table):
        source = jnp.broadcast_to(values, position.shape)
        found = jnp.take_along_axis(source, lane, axis=1, mode="promise_in_bounds")
        out = jnp.where(row == r, found, out)
    return out


def position_offset(columns):
    ocean = lax.axis_size("sec") - 1
    return jnp.where(lax.axis_index("sec") == ocean, 0, ocean * columns)


def edge_sources():
    section, tile = lax.axis_index("sec"), lax.axis_index("tile")
    sections = lax.axis_size("sec")
    other = section + sections // 2
    other = jnp.where(other >= sections, other - sections, other)
    last = lax.axis_size("tile") - 1
    return jnp.where(tile == last, other, section), jnp.where(tile == 0, other, section)


def even_tile():
    return lax.rem(lax.axis_index("tile"), 2) == 0


def sent_edges():
    up, down = edge_sources()
    even = even_tile()
    return (
        (jnp.where(even, down, up), jnp.where(even, 0, HALO)),
        (jnp.where(even, up, down), jnp.where(even, HALO, 0)),
    )


def sides(odd, even, start, rows):
    first, second = odd[start : start + rows, :], even[start : start + rows, :]
    here = even_tile()
    return jnp.where(here, first, second), jnp.where(here, second, first)


def lane_ids(shape):
    return lax.broadcasted_iota(jnp.int32, shape, len(shape) - 1)


def pack_edges(first, last):
    lane = lane_ids(first.shape)
    return jnp.where(lane < HALO, first, pltpu.roll(last, 2 * HALO, 1))


def prepare(state, tendency, diffusion, index, weight, out, *scratch):
    levels, columns = state.shape
    tail = columns - LANES
    *ends, bottom, indices, weights, sems = scratch
    pairs = []
    for ref, head, back in zip((state, diffusion, tendency), ends[::2], ends[1::2]):
        pairs.append((ref.at[:, pl.ds(0, LANES)], head))
        pairs.append((ref.at[:, pl.ds(tail, LANES)], back))
    pairs.append((state.at[pl.ds(levels - 8, 8), :], bottom))
    pairs.append((index, indices))
    pairs.append((weight, weights))
    copies = [
        pltpu.make_async_copy(source, target, sems.at[i])
        for i, (source, target) in enumerate(pairs)
    ]
    for copy in copies:
        copy.start()
    for copy in copies:
        copy.wait()
    block = jnp.zeros((levels, LANES), f32)
    lane = lane_ids(block.shape)
    for i in range(3):
        edges = pack_edges(ends[2 * i][...].astype(f32), ends[2 * i + 1][...].astype(f32))
        if i:
            edges = pltpu.roll(edges, 2 * HALO * i, 1)
        inside = (lane >= 2 * HALO * i) & (lane < 2 * HALO * (i + 1))
        block = jnp.where(inside, edges, block)
    out[0:48, :] = block.T[0:48, :]
    for j in range(columns // LANES):
        out[48 + j : 49 + j, :] = bottom[7:8, j * LANES : (j + 1) * LANES]
    out[52:56, :] = pack_edges(weights[:, :LANES], weights[:, tail:])
    position = (indices[...] + position_offset(columns)).astype(f32)
    out[56:60, :] = pack_edges(position[:, :LANES], position[:, tail:])
    out[60:64, :] = jnp.zeros((4, LANES), f32)


def edge_boundary(table, shared, surface_first, surface_last, source):
    position = shared[source, 56:60, :].astype(jnp.int32)
    picked = pick(table, position)
    partner = jnp.sum(shared[source, 52:56, :] * picked, axis=0, keepdims=True)
    return partner - pack_edges(surface_first, surface_last)


def own_boundary(table, index, weight, surface, out):
    offset = position_offset(out.shape[1])
    for j in range(out.shape[1] // LANES):
        cut = slice(j * LANES, (j + 1) * LANES)
        picked = pick(table, index[:, cut] + offset)
        partner = jnp.sum(weight[:, cut] * picked, axis=0, keepdims=True)
        out[:, cut] = partner - surface(j)


def couple_first(
    shared, index, weight, slots, weights, counts, boundary, odd, lists, even
):
    steps, ranks, occultations = slots.shape
    for p in range(steps):
        rank = lax.broadcasted_iota(jnp.int32, (ranks, occultations), 0)
        lists[p * ranks : (p + 1) * ranks, :] = slots[p].astype(f32)
        live = jnp.where(rank < counts[p : p + 1, :], weights[p], 0.0)
        lists[(steps + p) * ranks : (steps + p + 1) * ranks, :] = live
    section = lax.axis_index("sec")
    table = [shared[s, r : r + 1, :] for s in range(shared.shape[0]) for r in range(48, 52)]
    own_boundary(
        table, index, weight, lambda j: shared[section, 48 + j : 49 + j, :], boundary
    )
    for out, (source, start) in zip((odd, even), sent_edges()):
        for i in range(3):
            row = pl.multiple_of(2 * HALO * i + start, HALO)
            out[HALO * i : HALO * (i + 1), :] = shared[source, pl.ds(row, HALO), :]
        edge = edge_boundary(
            table, shared, shared[source, 48:49, :], shared[source, 51:52, :], source
        )
        out[24:32, :] = jnp.broadcast_to(edge, (8, LANES))


def couple_second(surfaces, shared, index, weight, boundary, odd, even):
    section = lax.axis_index("sec")
    table = [surfaces[s, r : r + 1, :] for s in range(surfaces.shape[0]) for r in range(4)]
    own_boundary(
        table, index, weight, lambda j: surfaces[section, j : j + 1, :], boundary
    )
    for out, (source, _) in zip((odd, even), sent_edges()):
        edge = edge_boundary(
            table, shared, surfaces[source, 0:1, :], surfaces[source, 3:4, :], source
        )
        out[...] = jnp.broadcast_to(edge, out.shape)


def edge_row(low, high):
    return jnp.where(lane_ids(low.shape) < HALO, high, low)


def halo_rows(odd, even, start):
    low, high = sides(odd, even, start, HALO)
    return jnp.concatenate([high, low], axis=0)


def turned(x):
    x = x.astype(f32)
    return [x[:, j * LANES : (j + 1) * LANES].T for j in range(x.shape[1] // LANES)]


def advance(field, rates, constant, right, alive):
    count = field.shape[0]
    live = alive[...] > 0.0
    for _ in range(SUBS):
        near = pltpu.roll(field, 1, 0) + pltpu.roll(field, count - 1, 0)
        spread = field + rates * (near - 2.0 * field)
        stepped = matmul(left_operand(spread), right) + constant
        field = jnp.where(live, stepped, field)
    return field


def forcing(response, boundary, edge, tendency):
    count = boundary.shape[1] // LANES
    rows = [boundary[:, j * LANES : (j + 1) * LANES] for j in range(count)]
    rows += [edge, jnp.zeros((7 - count, LANES), f32)]
    values = jnp.concatenate(rows, axis=0).T
    parts = [values[:, j : j + 1] * response for j in range(count)]
    parts.append(values[: 2 * HALO, count : count + 1] * response)
    return jnp.concatenate(parts, axis=0) + tendency


def one_hot(listed, columns):
    return jnp.concatenate(
        [
            jnp.where(listed[:, m : m + 1] == lane_ids((listed.shape[0], columns)), 1.0, 0.0)
            for m in range(listed.shape[1])
        ],
        axis=0,
    ).astype(bf16)


def chosen(field, hits):
    high, low = halves(field)
    both = matmul(hits, jnp.concatenate([high, low], axis=1))
    levels = field.shape[1]
    both = both[:, :levels] + both[:, levels:]
    tiles = hits.shape[0] // 4
    return [both[m * tiles : (m + 1) * tiles] for m in range(4)]


def step_first(
    state, tendency, diffusion, right, response, alive, boundary, odd, even,
    window, rates_out, forcing_out, surface,
):
    rates = jnp.concatenate(turned(diffusion[...]) + [halo_rows(odd, even, 8)], axis=0)
    tend = jnp.concatenate(turned(tendency[...]) + [halo_rows(odd, even, 16)], axis=0)
    field = jnp.concatenate(turned(state[...]) + [halo_rows(odd, even, 0)], axis=0)
    edge = edge_row(*sides(odd, even, 24, 1))
    constant = forcing(response[0:1, :], boundary, edge, tend)
    rates_out[...] = rates
    forcing_out[...] = tend
    field = advance(field, rates, constant, right[...], alive)
    window[...] = field
    for j in range(surface.shape[0]):
        block = field[j * LANES : (j + 1) * LANES].T
        surface[j : j + 1, :] = block[block.shape[0] - 1 :, :]


def step_second(
    window, rates, tend, right, response, alive, hits, boundary, odd, even, earlier,
    final, parcels,
):
    edge = edge_row(*sides(odd, even, 0, 1))
    constant = forcing(response[0:1, :], boundary, edge, tend[...])
    field = advance(window[...], rates[...], constant, right[...], alive)
    columns = final.shape[1]
    slots, tiles, _ = earlier.shape
    part = tiles // PARTS
    width = PARTS * STEPS * slots
    for m, later in enumerate(chosen(field[:columns], hits[...])):
        for o in range(PARTS):
            for p, rows in enumerate((earlier[m], later)):
                first = (o * STEPS + p) * slots + m
                owned = rows[o * part : (o + 1) * part]
                parcels[pl.ds(first, part, stride=width), :] = owned
    for j in range(columns // LANES):
        cut = slice(j * LANES, (j + 1) * LANES)
        final[:, cut] = field[cut].T


def ready_first(active, mixing, coupling, right, response, alive):
    right[...] = right_operand(mixing[...].T)
    response[...] = jnp.broadcast_to(coupling[...], response.shape)
    row = lax.broadcasted_iota(jnp.int32, alive.shape, 0)
    columns = alive.shape[0] - 2 * HALO
    column = jnp.where(row < columns, row, row - columns)
    column = jnp.where(row < columns + HALO, column, row - 2 * HALO)
    alive[...] = jnp.where(column < active[lax.axis_index("sec")], 1.0, 0.0)


def ready_second(
    listed, window, lists, mirrored, refraction, abel, hits, parcel, spread, right, right_abel
):
    columns = hits.shape[1]
    slots = parcel.shape[0]
    places = jnp.concatenate([listed[p] for p in range(STEPS)], axis=0).T
    for m, rows in enumerate(
        chosen(window[0:columns, :], one_hot(places[:, :slots], columns))
    ):
        parcel[m] = rows
    hits[...] = one_hot(places[:, slots : 2 * slots], columns)
    right[...] = right_operand(refraction[...])
    right_abel[...] = right_operand(abel[...])
    occultations, width = spread.shape[2], spread.shape[3] // 3
    ranks = lists.shape[0] // (2 * STEPS)
    part = width // 4
    here = jnp.where(lax.axis_index("tile") >= part, 1, 0)
    place = lane_ids((occultations, width))
    for o in range(PARTS):
        owned = jnp.where(here == o, lists[...], mirrored[...])
        for p in range(STEPS):
            slot = owned[p * ranks : (p + 1) * ranks].astype(jnp.int32)
            live = owned[(STEPS + p) * ranks : (STEPS + p + 1) * ranks].T
            source = (slot >> 2) - here * part
            inside = (source >= 0) & (source < part)
            key = jnp.where(inside, (slot & 3) * part + source, -1).T
            total = jnp.zeros((occultations, width), f32)
            for k in range(ranks):
                hit = key[:, k : k + 1] == place
                total = total + jnp.where(hit, live[:, k : k + 1], 0.0)
            spread[o, p] = left_operand(total)


def project(arrived, spread, refraction, kept, sent):
    occultations, width = spread.shape[2:]
    part = width // 12
    profiles = []
    for o in range(PARTS):
        for p in range(STEPS):
            first = 4 * (o * STEPS + p)
            values = jnp.concatenate(
                [
                    arrived[pl.ds(first + m, part, stride=4 * PARTS * STEPS), :]
                    for m in range(4)
                ],
                axis=0,
            )
            profiles.append(matmul(spread[o, p], right_operand(values)))
    profile = jnp.concatenate(profiles, axis=0)
    projected = matmul(left_operand(profile), refraction[...])
    pairs = kept.shape[0] // PARTS
    rows = occultations // (2 * pairs)
    first_core = lax.rem(lax.axis_index("sec"), 2) == 0
    for o in range(PARTS):
        for p in range(STEPS):
            for pair in range(pairs):
                start = (o * STEPS + p) * occultations + 2 * pair * rows
                low = projected[start : start + rows]
                high = projected[start + rows : start + 2 * rows]
                target = (pair * PARTS + o, slice(p * rows, (p + 1) * rows))
                kept[target] = jnp.where(first_core, low, high)
                sent[target] = jnp.where(first_core, high, low)


def depart(received, abel, observed, out):
    total = received[0]
    for s in range(1, received.shape[0]):
        total = total + received[s]
    bending = matmul(left_operand(total), abel[...])
    steps, rows, _ = observed.shape
    for p in range(steps):
        out[p] = observed[p] - bending[p * rows : (p + 1) * rows, :]


def shards(
    state,
    tendency,
    diffusion,
    mixing,
    coupling,
    remap_index,
    remap_weight,
    active_cols,
    send_cols,
    occ_slot,
    occ_weight,
    occ_count,
    refraction,
    abel_matrix,
    observed,
):
    sections = lax.axis_size("sec")
    tiles = lax.axis_size("tile")
    levels, columns = state.shape[1:]
    rows, heights = observed.shape[1:]
    width = columns + 2 * HALO
    half = sections // 2
    part = tiles // PARTS
    ranks, owned = occ_slot.shape[2:]
    swaps = ([], [])
    for s in range(sections):
        for t in range(tiles):
            target = ((s + half) % sections if t == tiles - 1 else s) * tiles + (t + 1) % tiles
            swaps[t % 2].extend([(s * tiles + t, target), (target, s * tiles + t)])
    above_even, above_odd = swaps
    listed = jnp.transpose(send_cols[:, 0, 0], (0, 2, 1))
    index, weight = remap_index[0], remap_weight[0]
    shape = jax.ShapeDtypeStruct
    after = lax.optimization_barrier

    edges = call(
        prepare,
        shape((64, LANES), f32),
        *(
            pltpu.with_memory_space_constraint(x, pltpu.HBM)
            for x in (state[0], tendency[0], diffusion[0], index, weight)
        ),
        space=pltpu.HBM,
        scratch=[pltpu.VMEM((levels, LANES), f32)] * 2
        + [pltpu.VMEM((levels, LANES), bf16)] * 4
        + [
            pltpu.VMEM((8, columns), f32),
            pltpu.VMEM(index.shape, jnp.int32),
            pltpu.VMEM(weight.shape, f32),
            pltpu.SemaphoreType.DMA((9,)),
        ],
    )
    shared = lax.all_gather(edges, "sec", axis=0, tiled=False)
    boundary, odd, lists, even = call(
        couple_first,
        (
            shape((1, columns), f32),
            shape((32, LANES), f32),
            shape((2 * STEPS * ranks, owned), f32),
            shape((32, LANES), f32),
        ),
        shared, index, weight, occ_slot[:, 0], occ_weight[:, 0], occ_count[:, 0],
    )
    odd = lax.ppermute(odd, AXES, above_odd)
    mirrored = lax.ppermute(lists, "tile", [(t, (t + part) % tiles) for t in range(tiles)])
    even = lax.ppermute(even, AXES, above_even)
    mixing_row, _ = after((mixing[0], boundary))
    right, response, alive = call(
        ready_first,
        (
            shape((3 * levels, levels), bf16),
            shape((8, levels), f32),
            shape((width, levels), f32),
        ),
        active_cols, mixing_row, coupling,
    )
    window, rates, tend, surface = call(
        step_first,
        (
            shape((width, levels), f32),
            shape((width, levels), f32),
            shape((width, levels), f32),
            shape((columns // LANES, LANES), f32),
        ),
        state[0], tendency[0], diffusion[0], right, response, alive, boundary, odd, even,
    )
    surfaces = lax.all_gather(surface, "sec", axis=0, tiled=False)
    boundary, odd, even = call(
        couple_second,
        (shape((1, columns), f32), shape((8, LANES), f32), shape((8, LANES), f32)),
        surfaces, shared, index, weight,
    )
    odd = lax.ppermute(odd, AXES, above_odd)
    even = lax.ppermute(even, AXES, above_even)
    mirrored, _ = after((mirrored, boundary))
    hits, parcel, spread, refract, bend = call(
        ready_second,
        (
            shape((4 * tiles, columns), bf16),
            shape((4, tiles, levels), f32),
            shape((PARTS, STEPS, owned, 12 * part), bf16),
            shape((3 * levels, levels), bf16),
            shape((3 * levels, heights), bf16),
        ),
        listed, window, lists, mirrored, refraction[0], abel_matrix,
    )
    final, parcels = call(
        step_second,
        (shape((levels, columns), f32), shape((8 * tiles, levels), f32)),
        window, rates, tend, right, response, alive, hits, boundary, odd, even, parcel,
    )
    parcels, spread, refract, bend = after((parcels, spread, refract, bend))
    arrived = lax.all_to_all(
        parcels.reshape(part, 8 * PARTS, levels),
        "tile",
        split_axis=0,
        concat_axis=0,
        axis_index_groups=[[o * part + i for i in range(part)] for o in range(PARTS)],
        tiled=True,
    )
    block = shape((half * PARTS, STEPS * rows, levels), f32)
    kept, sent = call(
        project, (block, block), arrived.reshape(8 * PARTS * part, levels), spread, refract
    )
    got = lax.ppermute(sent, "sec", [(s, s ^ 1) for s in range(sections)])
    received = lax.all_to_all(
        kept + got,
        AXES,
        split_axis=0,
        concat_axis=0,
        axis_index_groups=[
            [(2 * z + core) * tiles + o * part + i for z in range(half) for o in range(PARTS)]
            for core in range(2)
            for i in range(part)
        ],
        tiled=True,
    )
    departures = call(
        depart, shape((STEPS, rows, heights), f32), received, bend, observed
    )
    return (final[None], departures)


def solution(mesh):
    return jax.shard_map(
        shards,
        mesh=mesh,
        in_specs=(
            P("sec", None, "tile"),
            P("sec", None, "tile"),
            P("sec", None, "tile"),
            P("sec", None, None),
            P("sec", None),
            P("sec", None, "tile"),
            P("sec", None, "tile"),
            P(),
            P(None, "sec", "tile", None, None),
            P(None, "sec", None, "tile"),
            P(None, "sec", None, "tile"),
            P(None, "sec", "tile"),
            P("sec", None, None),
            P(),
            P(None, ("sec", "tile"), None),
        ),
        out_specs=(P("sec", None, "tile"), P(None, ("sec", "tile"), None)),
        check_vma=False,
    )
```

```python
import jax
import jax.numpy as jnp
from jax import lax
from jax.experimental import pallas as pl
from jax.experimental.pallas import tpu as pltpu
from jax.sharding import PartitionSpec as P

SUBS = 4
STEPS = 2
PARTS = 2
HALO = 8
LANES = 128
AXES = ("sec", "tile")
f32 = jnp.float32
bf16 = jnp.bfloat16


def call(body, outs, *args, scratch=(), space=pltpu.VMEM):
    in_specs = [
        pl.BlockSpec(memory_space=pltpu.SMEM if a.ndim == 1 else space) for a in args
    ]
    single = not isinstance(outs, (tuple, list))
    specs = pl.BlockSpec(memory_space=pltpu.VMEM)
    return pl.pallas_call(
        body,
        out_shape=outs if single else tuple(outs),
        in_specs=in_specs,
        out_specs=specs if single else tuple(specs for _ in outs),
        scratch_shapes=list(scratch),
        compiler_params=pltpu.CompilerParams(vmem_limit_bytes=40 * 2**20),
    )(*args)


def halves(x):
    high = x.astype(bf16)
    return high, (x - high.astype(f32)).astype(bf16)


def left_operand(x):
    high, low = halves(x)
    return jnp.concatenate([high, high, low], axis=1)


def right_operand(x):
    high, low = halves(x)
    return jnp.concatenate([high, low, high], axis=0)


def matmul(left, right):
    return jnp.dot(left, right, preferred_element_type=f32)


def pick(table, position):
    lane = position & (LANES - 1)
    row = position >> 7
    out = jnp.zeros(position.shape, f32)
    for r, values in enumerate(table):
        source = jnp.broadcast_to(values, position.shape)
        found = jnp.take_along_axis(source, lane, axis=1, mode="promise_in_bounds")
        out = jnp.where(row == r, found, out)
    return out


def position_offset(columns):
    ocean = lax.axis_size("sec") - 1
    return jnp.where(lax.axis_index("sec") == ocean, 0, ocean * columns)


def edge_sources():
    section, tile = lax.axis_index("sec"), lax.axis_index("tile")
    sections = lax.axis_size("sec")
    other = section + sections // 2
    other = jnp.where(other >= sections, other - sections, other)
    last = lax.axis_size("tile") - 1
    return jnp.where(tile == last, other, section), jnp.where(tile == 0, other, section)


def even_tile():
    return lax.rem(lax.axis_index("tile"), 2) == 0


def sent_edges():
    up, down = edge_sources()
    even = even_tile()
    return (
        (jnp.where(even, down, up), jnp.where(even, 0, HALO)),
        (jnp.where(even, up, down), jnp.where(even, HALO, 0)),
    )


def sides(odd, even, start, rows):
    first, second = odd[start : start + rows, :], even[start : start + rows, :]
    here = even_tile()
    return jnp.where(here, first, second), jnp.where(here, second, first)


def lane_ids(shape):
    return lax.broadcasted_iota(jnp.int32, shape, len(shape) - 1)


def pack_edges(first, last):
    lane = lane_ids(first.shape)
    return jnp.where(lane < HALO, first, pltpu.roll(last, 2 * HALO, 1))


def prepare(state, tendency, diffusion, index, weight, out, *scratch):
    levels, columns = state.shape
    tail = columns - LANES
    *ends, bottom, indices, weights, sems = scratch
    pairs = []
    for ref, head, back in zip((state, diffusion, tendency), ends[::2], ends[1::2]):
        pairs.append((ref.at[:, pl.ds(0, LANES)], head))
        pairs.append((ref.at[:, pl.ds(tail, LANES)], back))
    pairs.append((state.at[pl.ds(levels - 8, 8), :], bottom))
    pairs.append((index, indices))
    pairs.append((weight, weights))
    copies = [
        pltpu.make_async_copy(source, target, sems.at[i])
        for i, (source, target) in enumerate(pairs)
    ]
    for copy in copies:
        copy.start()
    for copy in copies:
        copy.wait()
    block = jnp.zeros((levels, LANES), f32)
    lane = lane_ids(block.shape)
    for i in range(3):
        edges = pack_edges(ends[2 * i][...].astype(f32), ends[2 * i + 1][...].astype(f32))
        if i:
            edges = pltpu.roll(edges, 2 * HALO * i, 1)
        inside = (lane >= 2 * HALO * i) & (lane < 2 * HALO * (i + 1))
        block = jnp.where(inside, edges, block)
    out[0:48, :] = block.T[0:48, :]
    for j in range(columns // LANES):
        out[48 + j : 49 + j, :] = bottom[7:8, j * LANES : (j + 1) * LANES]
    out[52:56, :] = pack_edges(weights[:, :LANES], weights[:, tail:])
    position = (indices[...] + position_offset(columns)).astype(f32)
    out[56:60, :] = pack_edges(position[:, :LANES], position[:, tail:])
    out[60:64, :] = jnp.zeros((4, LANES), f32)


def edge_boundary(table, shared, surface_first, surface_last, source):
    position = shared[source, 56:60, :].astype(jnp.int32)
    picked = pick(table, position)
    partner = jnp.sum(shared[source, 52:56, :] * picked, axis=0, keepdims=True)
    return partner - pack_edges(surface_first, surface_last)


def own_boundary(table, index, weight, surface, out):
    offset = position_offset(out.shape[1])
    for j in range(out.shape[1] // LANES):
        cut = slice(j * LANES, (j + 1) * LANES)
        picked = pick(table, index[:, cut] + offset)
        partner = jnp.sum(weight[:, cut] * picked, axis=0, keepdims=True)
        out[:, cut] = partner - surface(j)


def couple_first(
    shared, index, weight, slots, weights, counts, boundary, odd, lists, even
):
    steps, ranks, occultations = slots.shape
    for p in range(steps):
        rank = lax.broadcasted_iota(jnp.int32, (ranks, occultations), 0)
        lists[p * ranks : (p + 1) * ranks, :] = slots[p].astype(f32)
        live = jnp.where(rank < counts[p : p + 1, :], weights[p], 0.0)
        lists[(steps + p) * ranks : (steps + p + 1) * ranks, :] = live
    section = lax.axis_index("sec")
    table = [shared[s, r : r + 1, :] for s in range(shared.shape[0]) for r in range(48, 52)]
    own_boundary(
        table, index, weight, lambda j: shared[section, 48 + j : 49 + j, :], boundary
    )
    for out, (source, start) in zip((odd, even), sent_edges()):
        for i in range(3):
            row = pl.multiple_of(2 * HALO * i + start, HALO)
            out[HALO * i : HALO * (i + 1), :] = shared[source, pl.ds(row, HALO), :]
        edge = edge_boundary(
            table, shared, shared[source, 48:49, :], shared[source, 51:52, :], source
        )
        out[24:32, :] = jnp.broadcast_to(edge, (8, LANES))


def couple_second(surfaces, shared, index, weight, boundary, odd, even):
    section = lax.axis_index("sec")
    table = [surfaces[s, r : r + 1, :] for s in range(surfaces.shape[0]) for r in range(4)]
    own_boundary(
        table, index, weight, lambda j: surfaces[section, j : j + 1, :], boundary
    )
    for out, (source, _) in zip((odd, even), sent_edges()):
        edge = edge_boundary(
            table, shared, surfaces[source, 0:1, :], surfaces[source, 3:4, :], source
        )
        out[...] = jnp.broadcast_to(edge, out.shape)


def edge_row(low, high):
    return jnp.where(lane_ids(low.shape) < HALO, high, low)


def halo_rows(odd, even, start):
    low, high = sides(odd, even, start, HALO)
    return jnp.concatenate([high, low], axis=0)


def turned(x):
    x = x.astype(f32)
    return [x[:, j * LANES : (j + 1) * LANES].T for j in range(x.shape[1] // LANES)]


def advance(field, rates, constant, right, alive):
    count = field.shape[0]
    live = alive[...] > 0.0
    for _ in range(SUBS):
        near = pltpu.roll(field, 1, 0) + pltpu.roll(field, count - 1, 0)
        spread = field + rates * (near - 2.0 * field)
        stepped = matmul(left_operand(spread), right) + constant
        field = jnp.where(live, stepped, field)
    return field


def forcing(response, boundary, edge, tendency):
    count = boundary.shape[1] // LANES
    rows = [boundary[:, j * LANES : (j + 1) * LANES] for j in range(count)]
    rows += [edge, jnp.zeros((7 - count, LANES), f32)]
    values = jnp.concatenate(rows, axis=0).T
    parts = [values[:, j : j + 1] * response for j in range(count)]
    parts.append(values[: 2 * HALO, count : count + 1] * response)
    return jnp.concatenate(parts, axis=0) + tendency


def one_hot(listed, columns):
    return jnp.concatenate(
        [
            jnp.where(listed[:, m : m + 1] == lane_ids((listed.shape[0], columns)), 1.0, 0.0)
            for m in range(listed.shape[1])
        ],
        axis=0,
    ).astype(bf16)


def chosen(field, hits):
    high, low = halves(field)
    both = matmul(hits, jnp.concatenate([high, low], axis=1))
    levels = field.shape[1]
    both = both[:, :levels] + both[:, levels:]
    tiles = hits.shape[0] // 4
    return [both[m * tiles : (m + 1) * tiles] for m in range(4)]


def place(parcels, period, picked):
    slots = len(picked)
    part = picked[0].shape[0] // PARTS
    width = PARTS * STEPS * slots
    for m, rows in enumerate(picked):
        for o in range(PARTS):
            first = (o * STEPS + period) * slots + m
            parcels[pl.ds(first, part, stride=width), :] = rows[o * part : (o + 1) * part]


def step_first(
    state, tendency, diffusion, right, response, alive, boundary, odd, even,
    window, rates_out, forcing_out, surface,
):
    rates = jnp.concatenate(turned(diffusion[...]) + [halo_rows(odd, even, 8)], axis=0)
    tend = jnp.concatenate(turned(tendency[...]) + [halo_rows(odd, even, 16)], axis=0)
    field = jnp.concatenate(turned(state[...]) + [halo_rows(odd, even, 0)], axis=0)
    edge = edge_row(*sides(odd, even, 24, 1))
    constant = forcing(response[0:1, :], boundary, edge, tend)
    rates_out[...] = rates
    forcing_out[...] = tend
    field = advance(field, rates, constant, right[...], alive)
    window[...] = field
    for j in range(surface.shape[0]):
        block = field[j * LANES : (j + 1) * LANES].T
        surface[j : j + 1, :] = block[block.shape[0] - 1 :, :]


def step_second(
    window, rates, tend, right, response, alive, hits, boundary, odd, even, earlier,
    last, parcels,
):
    edge = edge_row(*sides(odd, even, 0, 1))
    constant = forcing(response[0:1, :], boundary, edge, tend[...])
    field = advance(window[...], rates[...], constant, right[...], alive)
    own = field[: last.shape[0]]
    last[...] = own
    parcels[...] = earlier[...]
    place(parcels, 1, chosen(own, hits[...]))


def finish(last, final):
    for j in range(final.shape[1] // LANES):
        cut = slice(j * LANES, (j + 1) * LANES)
        final[:, cut] = last[cut, :].T


def ready_first(active, mixing, coupling, right, response, alive):
    right[...] = right_operand(mixing[...].T)
    response[...] = jnp.broadcast_to(coupling[...], response.shape)
    row = lax.broadcasted_iota(jnp.int32, alive.shape, 0)
    columns = alive.shape[0] - 2 * HALO
    column = jnp.where(row < columns, row, row - columns)
    column = jnp.where(row < columns + HALO, column, row - 2 * HALO)
    alive[...] = jnp.where(column < active[lax.axis_index("sec")], 1.0, 0.0)


def ready_second(
    listed, window, lists, mirrored, refraction, abel, hits, parcels, spread, right, right_abel
):
    columns = hits.shape[1]
    slots = listed.shape[1]
    places = jnp.concatenate([listed[p] for p in range(STEPS)], axis=0).T
    place(parcels, 0, chosen(window[0:columns, :], one_hot(places[:, :slots], columns)))
    hits[...] = one_hot(places[:, slots : 2 * slots], columns)
    right[...] = right_operand(refraction[...])
    right_abel[...] = right_operand(abel[...])
    occultations, width = spread.shape[2], spread.shape[3] // 3
    ranks = lists.shape[0] // (2 * STEPS)
    part = width // 4
    here = jnp.where(lax.axis_index("tile") >= part, 1, 0)
    position = lane_ids((occultations, width))
    for o in range(PARTS):
        owned = jnp.where(here == o, lists[...], mirrored[...])
        for p in range(STEPS):
            slot = owned[p * ranks : (p + 1) * ranks].astype(jnp.int32)
            live = owned[(STEPS + p) * ranks : (STEPS + p + 1) * ranks].T
            source = (slot >> 2) - here * part
            inside = (source >= 0) & (source < part)
            key = jnp.where(inside, (slot & 3) * part + source, -1).T
            total = jnp.zeros((occultations, width), f32)
            for k in range(ranks):
                hit = key[:, k : k + 1] == position
                total = total + jnp.where(hit, live[:, k : k + 1], 0.0)
            spread[o, p] = left_operand(total)


def project(arrived, spread, refraction, kept, sent):
    occultations, width = spread.shape[2:]
    part = width // 12
    profiles = []
    for o in range(PARTS):
        for p in range(STEPS):
            first = 4 * (o * STEPS + p)
            values = jnp.concatenate(
                [
                    arrived[pl.ds(first + m, part, stride=4 * PARTS * STEPS), :]
                    for m in range(4)
                ],
                axis=0,
            )
            profiles.append(matmul(spread[o, p], right_operand(values)))
    profile = jnp.concatenate(profiles, axis=0)
    projected = matmul(left_operand(profile), refraction[...])
    pairs = kept.shape[0] // PARTS
    rows = occultations // (2 * pairs)
    first_core = lax.rem(lax.axis_index("sec"), 2) == 0
    for o in range(PARTS):
        for p in range(STEPS):
            for pair in range(pairs):
                start = (o * STEPS + p) * occultations + 2 * pair * rows
                low = projected[start : start + rows]
                high = projected[start + rows : start + 2 * rows]
                target = (pair * PARTS + o, slice(p * rows, (p + 1) * rows))
                kept[target] = jnp.where(first_core, low, high)
                sent[target] = jnp.where(first_core, high, low)


def depart(received, abel, observed, out):
    total = received[0]
    for s in range(1, received.shape[0]):
        total = total + received[s]
    bending = matmul(left_operand(total), abel[...])
    steps, rows, _ = observed.shape
    for p in range(steps):
        out[p] = observed[p] - bending[p * rows : (p + 1) * rows, :]


def shards(
    state,
    tendency,
    diffusion,
    mixing,
    coupling,
    remap_index,
    remap_weight,
    active_cols,
    send_cols,
    occ_slot,
    occ_weight,
    occ_count,
    refraction,
    abel_matrix,
    observed,
):
    sections = lax.axis_size("sec")
    tiles = lax.axis_size("tile")
    levels, columns = state.shape[1:]
    rows, heights = observed.shape[1:]
    width = columns + 2 * HALO
    half = sections // 2
    part = tiles // PARTS
    ranks, owned = occ_slot.shape[2:]
    swaps = ([], [])
    for s in range(sections):
        for t in range(tiles):
            target = ((s + half) % sections if t == tiles - 1 else s) * tiles + (t + 1) % tiles
            swaps[t % 2].extend([(s * tiles + t, target), (target, s * tiles + t)])
    above_even, above_odd = swaps
    listed = jnp.transpose(send_cols[:, 0, 0], (0, 2, 1))
    index, weight = remap_index[0], remap_weight[0]
    shape = jax.ShapeDtypeStruct
    after = lax.optimization_barrier

    edges = call(
        prepare,
        shape((64, LANES), f32),
        *(
            pltpu.with_memory_space_constraint(x, pltpu.HBM)
            for x in (state[0], tendency[0], diffusion[0], index, weight)
        ),
        space=pltpu.HBM,
        scratch=[pltpu.VMEM((levels, LANES), f32)] * 2
        + [pltpu.VMEM((levels, LANES), bf16)] * 4
        + [
            pltpu.VMEM((8, columns), f32),
            pltpu.VMEM(index.shape, jnp.int32),
            pltpu.VMEM(weight.shape, f32),
            pltpu.SemaphoreType.DMA((9,)),
        ],
    )
    shared = lax.all_gather(edges, "sec", axis=0, tiled=False)
    boundary, odd, lists, even = call(
        couple_first,
        (
            shape((1, columns), f32),
            shape((32, LANES), f32),
            shape((2 * STEPS * ranks, owned), f32),
            shape((32, LANES), f32),
        ),
        shared, index, weight, occ_slot[:, 0], occ_weight[:, 0], occ_count[:, 0],
    )
    odd = lax.ppermute(odd, AXES, above_odd)
    mirrored = lax.ppermute(lists, "tile", [(t, (t + part) % tiles) for t in range(tiles)])
    even = lax.ppermute(even, AXES, above_even)
    mixing_row, _ = after((mixing[0], boundary))
    right, response, alive = call(
        ready_first,
        (
            shape((3 * levels, levels), bf16),
            shape((8, levels), f32),
            shape((width, levels), f32),
        ),
        active_cols, mixing_row, coupling,
    )
    window, rates, tend, surface = call(
        step_first,
        (
            shape((width, levels), f32),
            shape((width, levels), f32),
            shape((width, levels), f32),
            shape((columns // LANES, LANES), f32),
        ),
        state[0], tendency[0], diffusion[0], right, response, alive, boundary, odd, even,
    )
    surfaces = lax.all_gather(surface, "sec", axis=0, tiled=False)
    boundary, odd, even = call(
        couple_second,
        (shape((1, columns), f32), shape((8, LANES), f32), shape((8, LANES), f32)),
        surfaces, shared, index, weight,
    )
    odd = lax.ppermute(odd, AXES, above_odd)
    even = lax.ppermute(even, AXES, above_even)
    mirrored, _ = after((mirrored, boundary))
    hits, parcels, spread, refract, bend = call(
        ready_second,
        (
            shape((4 * tiles, columns), bf16),
            shape((8 * tiles, levels), f32),
            shape((PARTS, STEPS, owned, 12 * part), bf16),
            shape((3 * levels, levels), bf16),
            shape((3 * levels, heights), bf16),
        ),
        listed, window, lists, mirrored, refraction[0], abel_matrix,
    )
    last, parcels = call(
        step_second,
        (shape((columns, levels), f32), shape((8 * tiles, levels), f32)),
        window, rates, tend, right, response, alive, hits, boundary, odd, even, parcels,
    )
    parcels, spread, refract, bend = after((parcels, spread, refract, bend))
    arrived = lax.all_to_all(
        parcels.reshape(part, 8 * PARTS, levels),
        "tile",
        split_axis=0,
        concat_axis=0,
        axis_index_groups=[[o * part + i for i in range(part)] for o in range(PARTS)],
        tiled=True,
    )
    block = shape((half * PARTS, STEPS * rows, levels), f32)
    kept, sent = call(
        project, (block, block), arrived.reshape(8 * PARTS * part, levels), spread, refract
    )
    got = lax.ppermute(sent, "sec", [(s, s ^ 1) for s in range(sections)])
    last, _ = after((last, kept))
    final = call(finish, shape((levels, columns), f32), last)
    got, final = after((got, final))
    received = lax.all_to_all(
        kept + got,
        AXES,
        split_axis=0,
        concat_axis=0,
        axis_index_groups=[
            [(2 * z + core) * tiles + o * part + i for z in range(half) for o in range(PARTS)]
            for core in range(2)
            for i in range(part)
        ],
        tiled=True,
    )
    departures = call(
        depart, shape((STEPS, rows, heights), f32), received, bend, observed
    )
    return (final[None], departures)


def solution(mesh):
    return jax.shard_map(
        shards,
        mesh=mesh,
        in_specs=(
            P("sec", None, "tile"),
            P("sec", None, "tile"),
            P("sec", None, "tile"),
            P("sec", None, None),
            P("sec", None),
            P("sec", None, "tile"),
            P("sec", None, "tile"),
            P(),
            P(None, "sec", "tile", None, None),
            P(None, "sec", None, "tile"),
            P(None, "sec", None, "tile"),
            P(None, "sec", "tile"),
            P("sec", None, None),
            P(),
            P(None, ("sec", "tile"), None),
        ),
        out_specs=(P("sec", None, "tile"), P(None, ("sec", "tile"), None)),
        check_vma=False,
    )
```

```python
import jax
import jax.numpy as jnp
from jax import lax
from jax.experimental import pallas as pl
from jax.experimental.pallas import tpu as pltpu
from jax.sharding import PartitionSpec as P

SUBS = 4
STEPS = 2
PARTS = 2
HALO = 8
LANES = 128
AXES = ("sec", "tile")
f32 = jnp.float32
bf16 = jnp.bfloat16


def call(body, outs, *args, scratch=(), space=pltpu.VMEM):
    in_specs = [
        pl.BlockSpec(memory_space=pltpu.SMEM if a.ndim == 1 else space) for a in args
    ]
    single = not isinstance(outs, (tuple, list))
    specs = pl.BlockSpec(memory_space=pltpu.VMEM)
    return pl.pallas_call(
        body,
        out_shape=outs if single else tuple(outs),
        in_specs=in_specs,
        out_specs=specs if single else tuple(specs for _ in outs),
        scratch_shapes=list(scratch),
        compiler_params=pltpu.CompilerParams(vmem_limit_bytes=40 * 2**20),
    )(*args)


def halves(x):
    high = x.astype(bf16)
    return high, (x - high.astype(f32)).astype(bf16)


def left_operand(x):
    high, low = halves(x)
    return jnp.concatenate([high, high, low], axis=1)


def right_operand(x):
    high, low = halves(x)
    return jnp.concatenate([high, low, high], axis=0)


def matmul(left, right):
    return jnp.dot(left, right, preferred_element_type=f32)


def pick(table, position):
    lane = position & (LANES - 1)
    row = position >> 7
    out = jnp.zeros(position.shape, f32)
    for r, values in enumerate(table):
        source = jnp.broadcast_to(values, position.shape)
        found = jnp.take_along_axis(source, lane, axis=1, mode="promise_in_bounds")
        out = jnp.where(row == r, found, out)
    return out


def position_offset(columns):
    ocean = lax.axis_size("sec") - 1
    return jnp.where(lax.axis_index("sec") == ocean, 0, ocean * columns)


def edge_sources():
    section, tile = lax.axis_index("sec"), lax.axis_index("tile")
    sections = lax.axis_size("sec")
    other = section + sections // 2
    other = jnp.where(other >= sections, other - sections, other)
    last = lax.axis_size("tile") - 1
    return jnp.where(tile == last, other, section), jnp.where(tile == 0, other, section)


def even_tile():
    return lax.rem(lax.axis_index("tile"), 2) == 0


def sent_edges():
    up, down = edge_sources()
    even = even_tile()
    return (
        (jnp.where(even, down, up), jnp.where(even, 0, HALO)),
        (jnp.where(even, up, down), jnp.where(even, HALO, 0)),
    )


def sides(odd, even, start, rows):
    first, second = odd[start : start + rows, :], even[start : start + rows, :]
    here = even_tile()
    return jnp.where(here, first, second), jnp.where(here, second, first)


def lane_ids(shape):
    return lax.broadcasted_iota(jnp.int32, shape, len(shape) - 1)


def pack_edges(first, last):
    lane = lane_ids(first.shape)
    return jnp.where(lane < HALO, first, pltpu.roll(last, 2 * HALO, 1))


def prepare(state, tendency, diffusion, index, weight, out, *scratch):
    levels, columns = state.shape
    tail = columns - LANES
    *ends, bottom, indices, weights, sems = scratch
    pairs = []
    for ref, head, back in zip((state, diffusion, tendency), ends[::2], ends[1::2]):
        pairs.append((ref.at[:, pl.ds(0, LANES)], head))
        pairs.append((ref.at[:, pl.ds(tail, LANES)], back))
    pairs.append((state.at[pl.ds(levels - 8, 8), :], bottom))
    pairs.append((index, indices))
    pairs.append((weight, weights))
    copies = [
        pltpu.make_async_copy(source, target, sems.at[i])
        for i, (source, target) in enumerate(pairs)
    ]
    for copy in copies:
        copy.start()
    for copy in copies:
        copy.wait()
    block = jnp.zeros((levels, LANES), f32)
    lane = lane_ids(block.shape)
    for i in range(3):
        edges = pack_edges(ends[2 * i][...].astype(f32), ends[2 * i + 1][...].astype(f32))
        if i:
            edges = pltpu.roll(edges, 2 * HALO * i, 1)
        inside = (lane >= 2 * HALO * i) & (lane < 2 * HALO * (i + 1))
        block = jnp.where(inside, edges, block)
    out[0:48, :] = block.T[0:48, :]
    for j in range(columns // LANES):
        out[48 + j : 49 + j, :] = bottom[7:8, j * LANES : (j + 1) * LANES]
    out[52:56, :] = pack_edges(weights[:, :LANES], weights[:, tail:])
    position = (indices[...] + position_offset(columns)).astype(f32)
    out[56:60, :] = pack_edges(position[:, :LANES], position[:, tail:])
    out[60:64, :] = jnp.zeros((4, LANES), f32)


def edge_boundary(table, shared, surface_first, surface_last, source):
    position = shared[source, 56:60, :].astype(jnp.int32)
    picked = pick(table, position)
    partner = jnp.sum(shared[source, 52:56, :] * picked, axis=0, keepdims=True)
    return partner - pack_edges(surface_first, surface_last)


def own_boundary(table, index, weight, surface, out):
    offset = position_offset(out.shape[1])
    for j in range(out.shape[1] // LANES):
        cut = slice(j * LANES, (j + 1) * LANES)
        picked = pick(table, index[:, cut] + offset)
        partner = jnp.sum(weight[:, cut] * picked, axis=0, keepdims=True)
        out[:, cut] = partner - surface(j)


def couple_first(
    shared, index, weight, slots, weights, counts, boundary, odd, lists, even
):
    steps, ranks, occultations = slots.shape
    for p in range(steps):
        rank = lax.broadcasted_iota(jnp.int32, (ranks, occultations), 0)
        lists[p * ranks : (p + 1) * ranks, :] = slots[p].astype(f32)
        live = jnp.where(rank < counts[p : p + 1, :], weights[p], 0.0)
        lists[(steps + p) * ranks : (steps + p + 1) * ranks, :] = live
    section = lax.axis_index("sec")
    table = [shared[s, r : r + 1, :] for s in range(shared.shape[0]) for r in range(48, 52)]
    own_boundary(
        table, index, weight, lambda j: shared[section, 48 + j : 49 + j, :], boundary
    )
    for out, (source, start) in zip((odd, even), sent_edges()):
        for i in range(3):
            row = pl.multiple_of(2 * HALO * i + start, HALO)
            out[HALO * i : HALO * (i + 1), :] = shared[source, pl.ds(row, HALO), :]
        edge = edge_boundary(
            table, shared, shared[source, 48:49, :], shared[source, 51:52, :], source
        )
        out[24:32, :] = jnp.broadcast_to(edge, (8, LANES))


def couple_second(surfaces, shared, index, weight, boundary, odd, even):
    section = lax.axis_index("sec")
    table = [surfaces[s, r : r + 1, :] for s in range(surfaces.shape[0]) for r in range(4)]
    own_boundary(
        table, index, weight, lambda j: surfaces[section, j : j + 1, :], boundary
    )
    for out, (source, _) in zip((odd, even), sent_edges()):
        edge = edge_boundary(
            table, shared, surfaces[source, 0:1, :], surfaces[source, 3:4, :], source
        )
        out[...] = jnp.broadcast_to(edge, out.shape)


def edge_row(low, high):
    return jnp.where(lane_ids(low.shape) < HALO, high, low)


def halo_rows(odd, even, start):
    low, high = sides(odd, even, start, HALO)
    return jnp.concatenate([high, low], axis=0)


def turned(x):
    x = x.astype(f32)
    return [x[:, j * LANES : (j + 1) * LANES].T for j in range(x.shape[1] // LANES)]


def advance(field, rates, constant, right, live_limit):
    count = field.shape[0]
    row = lax.broadcasted_iota(jnp.int32, field.shape, 0)
    columns = count - 2 * HALO
    column = jnp.where(row < columns, row, row - columns)
    live = jnp.where(row < columns + HALO, column, row - 2 * HALO) < live_limit
    for _ in range(SUBS):
        near = pltpu.roll(field, 1, 0) + pltpu.roll(field, count - 1, 0)
        spread = field + rates * (near - 2.0 * field)
        stepped = matmul(left_operand(spread), right) + constant
        field = jnp.where(live, stepped, field)
    return field


def forcing(response, boundary, edge, tendency):
    count = boundary.shape[1] // LANES
    rows = [boundary[:, j * LANES : (j + 1) * LANES] for j in range(count)]
    rows += [edge, jnp.zeros((7 - count, LANES), f32)]
    values = jnp.concatenate(rows, axis=0).T
    parts = [values[:, j : j + 1] * response for j in range(count)]
    parts.append(values[: 2 * HALO, count : count + 1] * response)
    return jnp.concatenate(parts, axis=0) + tendency


def one_hot(listed, columns):
    return jnp.concatenate(
        [
            jnp.where(listed[:, m : m + 1] == lane_ids((listed.shape[0], columns)), 1.0, 0.0)
            for m in range(listed.shape[1])
        ],
        axis=0,
    ).astype(bf16)


def chosen(field, hits):
    high, low = halves(field)
    both = matmul(hits, jnp.concatenate([high, low], axis=1))
    levels = field.shape[1]
    both = both[:, :levels] + both[:, levels:]
    tiles = hits.shape[0] // 4
    return [both[m * tiles : (m + 1) * tiles] for m in range(4)]


def place(parcels, period, picked):
    slots = len(picked)
    part = picked[0].shape[0] // PARTS
    width = PARTS * STEPS * slots
    for m, rows in enumerate(picked):
        for o in range(PARTS):
            first = (o * STEPS + period) * slots + m
            parcels[pl.ds(first, part, stride=width), :] = rows[o * part : (o + 1) * part]


def step_first(
    active, state, tendency, diffusion, mixing, coupling, boundary, odd, even,
    window, rates_out, forcing_out, surface, right, response,
):
    right[...] = right_operand(mixing[...].T)
    response[...] = jnp.broadcast_to(coupling[...], response.shape)
    rates = jnp.concatenate(turned(diffusion[...]) + [halo_rows(odd, even, 8)], axis=0)
    tend = jnp.concatenate(turned(tendency[...]) + [halo_rows(odd, even, 16)], axis=0)
    field = jnp.concatenate(turned(state[...]) + [halo_rows(odd, even, 0)], axis=0)
    edge = edge_row(*sides(odd, even, 24, 1))
    constant = forcing(response[0:1, :], boundary, edge, tend)
    rates_out[...] = rates
    forcing_out[...] = tend
    field = advance(field, rates, constant, right[...], active[lax.axis_index("sec")])
    window[...] = field
    for j in range(surface.shape[0]):
        block = field[j * LANES : (j + 1) * LANES].T
        surface[j : j + 1, :] = block[block.shape[0] - 1 :, :]


def step_second(
    active, window, rates, tend, right, response, hits, boundary, odd, even, earlier,
    last, parcels,
):
    edge = edge_row(*sides(odd, even, 0, 1))
    constant = forcing(response[0:1, :], boundary, edge, tend[...])
    live_limit = active[lax.axis_index("sec")]
    field = advance(window[...], rates[...], constant, right[...], live_limit)
    own = field[: last.shape[0]]
    last[...] = own
    parcels[...] = earlier[...]
    place(parcels, 1, chosen(own, hits[...]))


def finish(last, final):
    for j in range(final.shape[1] // LANES):
        cut = slice(j * LANES, (j + 1) * LANES)
        final[:, cut] = last[cut, :].T


def ready_second(
    listed, window, lists, mirrored, refraction, abel, hits, parcels, spread, right, right_abel
):
    columns = hits.shape[1]
    slots = listed.shape[1]
    places = jnp.concatenate([listed[p] for p in range(STEPS)], axis=0).T
    place(parcels, 0, chosen(window[0:columns, :], one_hot(places[:, :slots], columns)))
    hits[...] = one_hot(places[:, slots : 2 * slots], columns)
    right[...] = right_operand(refraction[...])
    right_abel[...] = right_operand(abel[...])
    occultations, width = spread.shape[2], spread.shape[3] // 3
    ranks = lists.shape[0] // (2 * STEPS)
    part = width // 4
    here = jnp.where(lax.axis_index("tile") >= part, 1, 0)
    position = lane_ids((occultations, width))
    for o in range(PARTS):
        owned = jnp.where(here == o, lists[...], mirrored[...])
        for p in range(STEPS):
            slot = owned[p * ranks : (p + 1) * ranks].astype(jnp.int32)
            live = owned[(STEPS + p) * ranks : (STEPS + p + 1) * ranks].T
            source = (slot >> 2) - here * part
            inside = (source >= 0) & (source < part)
            key = jnp.where(inside, (slot & 3) * part + source, -1).T
            total = jnp.zeros((occultations, width), f32)
            for k in range(ranks):
                hit = key[:, k : k + 1] == position
                total = total + jnp.where(hit, live[:, k : k + 1], 0.0)
            spread[o, p] = left_operand(total)


def project(arrived, spread, refraction, kept, sent):
    occultations, width = spread.shape[2:]
    part = width // 12
    profiles = []
    for o in range(PARTS):
        for p in range(STEPS):
            first = 4 * (o * STEPS + p)
            values = jnp.concatenate(
                [
                    arrived[pl.ds(first + m, part, stride=4 * PARTS * STEPS), :]
                    for m in range(4)
                ],
                axis=0,
            )
            profiles.append(matmul(spread[o, p], right_operand(values)))
    profile = jnp.concatenate(profiles, axis=0)
    projected = matmul(left_operand(profile), refraction[...])
    pairs = kept.shape[0] // PARTS
    rows = occultations // (2 * pairs)
    first_core = lax.rem(lax.axis_index("sec"), 2) == 0
    for o in range(PARTS):
        for p in range(STEPS):
            for pair in range(pairs):
                start = (o * STEPS + p) * occultations + 2 * pair * rows
                low = projected[start : start + rows]
                high = projected[start + rows : start + 2 * rows]
                target = (pair * PARTS + o, slice(p * rows, (p + 1) * rows))
                kept[target] = jnp.where(first_core, low, high)
                sent[target] = jnp.where(first_core, high, low)


def depart(received, abel, observed, out):
    total = received[0]
    for s in range(1, received.shape[0]):
        total = total + received[s]
    bending = matmul(left_operand(total), abel[...])
    steps, rows, _ = observed.shape
    for p in range(steps):
        out[p] = observed[p] - bending[p * rows : (p + 1) * rows, :]


def shards(
    state,
    tendency,
    diffusion,
    mixing,
    coupling,
    remap_index,
    remap_weight,
    active_cols,
    send_cols,
    occ_slot,
    occ_weight,
    occ_count,
    refraction,
    abel_matrix,
    observed,
):
    sections = lax.axis_size("sec")
    tiles = lax.axis_size("tile")
    levels, columns = state.shape[1:]
    rows, heights = observed.shape[1:]
    width = columns + 2 * HALO
    half = sections // 2
    part = tiles // PARTS
    ranks, owned = occ_slot.shape[2:]
    swaps = ([], [])
    for s in range(sections):
        for t in range(tiles):
            target = ((s + half) % sections if t == tiles - 1 else s) * tiles + (t + 1) % tiles
            swaps[t % 2].extend([(s * tiles + t, target), (target, s * tiles + t)])
    above_even, above_odd = swaps
    listed = jnp.transpose(send_cols[:, 0, 0], (0, 2, 1))
    index, weight = remap_index[0], remap_weight[0]
    shape = jax.ShapeDtypeStruct
    after = lax.optimization_barrier

    edges = call(
        prepare,
        shape((64, LANES), f32),
        *(
            pltpu.with_memory_space_constraint(x, pltpu.HBM)
            for x in (state[0], tendency[0], diffusion[0], index, weight)
        ),
        space=pltpu.HBM,
        scratch=[pltpu.VMEM((levels, LANES), f32)] * 2
        + [pltpu.VMEM((levels, LANES), bf16)] * 4
        + [
            pltpu.VMEM((8, columns), f32),
            pltpu.VMEM(index.shape, jnp.int32),
            pltpu.VMEM(weight.shape, f32),
            pltpu.SemaphoreType.DMA((9,)),
        ],
    )
    shared = lax.all_gather(edges, "sec", axis=0, tiled=False)
    boundary, odd, lists, even = call(
        couple_first,
        (
            shape((1, columns), f32),
            shape((32, LANES), f32),
            shape((2 * STEPS * ranks, owned), f32),
            shape((32, LANES), f32),
        ),
        shared, index, weight, occ_slot[:, 0], occ_weight[:, 0], occ_count[:, 0],
    )
    odd = lax.ppermute(odd, AXES, above_odd)
    mirrored = lax.ppermute(lists, "tile", [(t, (t + part) % tiles) for t in range(tiles)])
    even = lax.ppermute(even, AXES, above_even)
    window, rates, tend, surface, right, response = call(
        step_first,
        (
            shape((width, levels), f32),
            shape((width, levels), f32),
            shape((width, levels), f32),
            shape((columns // LANES, LANES), f32),
            shape((3 * levels, levels), bf16),
            shape((8, levels), f32),
        ),
        active_cols, state[0], tendency[0], diffusion[0], mixing[0], coupling, boundary, odd, even,
    )
    surfaces = lax.all_gather(surface, "sec", axis=0, tiled=False)
    boundary, odd, even = call(
        couple_second,
        (shape((1, columns), f32), shape((8, LANES), f32), shape((8, LANES), f32)),
        surfaces, shared, index, weight,
    )
    odd = lax.ppermute(odd, AXES, above_odd)
    even = lax.ppermute(even, AXES, above_even)
    mirrored, _ = after((mirrored, boundary))
    hits, parcels, spread, refract, bend = call(
        ready_second,
        (
            shape((4 * tiles, columns), bf16),
            shape((8 * tiles, levels), f32),
            shape((PARTS, STEPS, owned, 12 * part), bf16),
            shape((3 * levels, levels), bf16),
            shape((3 * levels, heights), bf16),
        ),
        listed, window, lists, mirrored, refraction[0], abel_matrix,
    )
    last, parcels = call(
        step_second,
        (shape((columns, levels), f32), shape((8 * tiles, levels), f32)),
        active_cols, window, rates, tend, right, response, hits, boundary, odd, even, parcels,
    )
    parcels, spread, refract, bend = after((parcels, spread, refract, bend))
    arrived = lax.all_to_all(
        parcels.reshape(part, 8 * PARTS, levels),
        "tile",
        split_axis=0,
        concat_axis=0,
        axis_index_groups=[[o * part + i for i in range(part)] for o in range(PARTS)],
        tiled=True,
    )
    block = shape((half * PARTS, STEPS * rows, levels), f32)
    kept, sent = call(
        project, (block, block), arrived.reshape(8 * PARTS * part, levels), spread, refract
    )
    got = lax.ppermute(sent, "sec", [(s, s ^ 1) for s in range(sections)])
    last, _ = after((last, kept))
    final = call(finish, shape((levels, columns), f32), last)
    got, final = after((got, final))
    received = lax.all_to_all(
        kept + got,
        AXES,
        split_axis=0,
        concat_axis=0,
        axis_index_groups=[
            [(2 * z + core) * tiles + o * part + i for z in range(half) for o in range(PARTS)]
            for core in range(2)
            for i in range(part)
        ],
        tiled=True,
    )
    departures = call(
        depart, shape((STEPS, rows, heights), f32), received, bend, observed
    )
    return (final[None], departures)


def solution(mesh):
    return jax.shard_map(
        shards,
        mesh=mesh,
        in_specs=(
            P("sec", None, "tile"),
            P("sec", None, "tile"),
            P("sec", None, "tile"),
            P("sec", None, None),
            P("sec", None),
            P("sec", None, "tile"),
            P("sec", None, "tile"),
            P(),
            P(None, "sec", "tile", None, None),
            P(None, "sec", None, "tile"),
            P(None, "sec", None, "tile"),
            P(None, "sec", "tile"),
            P("sec", None, None),
            P(),
            P(None, ("sec", "tile"), None),
        ),
        out_specs=(P("sec", None, "tile"), P(None, ("sec", "tile"), None)),
        check_vma=False,
    )
```

```python
import jax
import jax.numpy as jnp
from jax import lax
from jax.experimental import pallas as pl
from jax.experimental.pallas import tpu as pltpu
from jax.sharding import PartitionSpec as P

SUBS = 4
STEPS = 2
PARTS = 2
HALO = 8
LANES = 128
AXES = ("sec", "tile")
f32 = jnp.float32
bf16 = jnp.bfloat16


def call(body, outs, *args, scratch=(), space=pltpu.VMEM):
    in_specs = [
        pl.BlockSpec(memory_space=pltpu.SMEM if a.ndim == 1 else space) for a in args
    ]
    single = not isinstance(outs, (tuple, list))
    specs = pl.BlockSpec(memory_space=pltpu.VMEM)
    return pl.pallas_call(
        body,
        out_shape=outs if single else tuple(outs),
        in_specs=in_specs,
        out_specs=specs if single else tuple(specs for _ in outs),
        scratch_shapes=list(scratch),
        compiler_params=pltpu.CompilerParams(vmem_limit_bytes=40 * 2**20),
    )(*args)


def halves(x):
    high = x.astype(bf16)
    return high, (x - high.astype(f32)).astype(bf16)


def left_operand(x):
    high, low = halves(x)
    return jnp.concatenate([high, high, low], axis=1)


def right_operand(x):
    high, low = halves(x)
    return jnp.concatenate([high, low, high], axis=0)


def matmul(left, right):
    return jnp.dot(left, right, preferred_element_type=f32)


def pick(table, position):
    lane = position & (LANES - 1)
    row = position >> 7
    out = jnp.zeros(position.shape, f32)
    for r, values in enumerate(table):
        source = jnp.broadcast_to(values, position.shape)
        found = jnp.take_along_axis(source, lane, axis=1, mode="promise_in_bounds")
        out = jnp.where(row == r, found, out)
    return out


def position_offset(columns):
    ocean = lax.axis_size("sec") - 1
    return jnp.where(lax.axis_index("sec") == ocean, 0, ocean * columns)


def edge_sources():
    section, tile = lax.axis_index("sec"), lax.axis_index("tile")
    sections = lax.axis_size("sec")
    other = section + sections // 2
    other = jnp.where(other >= sections, other - sections, other)
    last = lax.axis_size("tile") - 1
    return jnp.where(tile == last, other, section), jnp.where(tile == 0, other, section)


def even_tile():
    return lax.rem(lax.axis_index("tile"), 2) == 0


def sent_edges():
    up, down = edge_sources()
    even = even_tile()
    return (
        (jnp.where(even, down, up), jnp.where(even, 0, HALO)),
        (jnp.where(even, up, down), jnp.where(even, HALO, 0)),
    )


def sides(odd, even, start, rows):
    first, second = odd[start : start + rows, :], even[start : start + rows, :]
    here = even_tile()
    return jnp.where(here, first, second), jnp.where(here, second, first)


def lane_ids(shape):
    return lax.broadcasted_iota(jnp.int32, shape, len(shape) - 1)


def pack_edges(first, last):
    lane = lane_ids(first.shape)
    return jnp.where(lane < HALO, first, pltpu.roll(last, 2 * HALO, 1))


def prepare(
    state, tendency, diffusion, index, weight, slot, share, count, out, lists, *scratch
):
    levels, columns = state.shape
    tail = columns - LANES
    *ends, bottom, indices, weights, slots, shares, counts, sems = scratch
    pairs = []
    for ref, head, back in zip((state, diffusion, tendency), ends[::2], ends[1::2]):
        pairs.append((ref.at[:, pl.ds(0, LANES)], head))
        pairs.append((ref.at[:, pl.ds(tail, LANES)], back))
    pairs.append((state.at[pl.ds(levels - 8, 8), :], bottom))
    pairs.append((index, indices))
    pairs.append((weight, weights))
    pairs.append((slot, slots))
    pairs.append((share, shares))
    pairs.append((count, counts))
    copies = [
        pltpu.make_async_copy(source, target, sems.at[i])
        for i, (source, target) in enumerate(pairs)
    ]
    for copy in copies:
        copy.start()
    for copy in copies:
        copy.wait()
    steps, ranks, occultations = slots.shape
    for p in range(steps):
        rank = lax.broadcasted_iota(jnp.int32, (ranks, occultations), 0)
        lists[p * ranks : (p + 1) * ranks, :] = slots[p].astype(f32)
        live = jnp.where(rank < counts[p : p + 1, :], shares[p], 0.0)
        lists[(steps + p) * ranks : (steps + p + 1) * ranks, :] = live
    block = jnp.zeros((levels, LANES), f32)
    lane = lane_ids(block.shape)
    for i in range(3):
        edges = pack_edges(ends[2 * i][...].astype(f32), ends[2 * i + 1][...].astype(f32))
        if i:
            edges = pltpu.roll(edges, 2 * HALO * i, 1)
        inside = (lane >= 2 * HALO * i) & (lane < 2 * HALO * (i + 1))
        block = jnp.where(inside, edges, block)
    out[0:48, :] = block.T[0:48, :]
    for j in range(columns // LANES):
        out[48 + j : 49 + j, :] = bottom[7:8, j * LANES : (j + 1) * LANES]
    out[52:56, :] = pack_edges(weights[:, :LANES], weights[:, tail:])
    position = (indices[...] + position_offset(columns)).astype(f32)
    out[56:60, :] = pack_edges(position[:, :LANES], position[:, tail:])
    out[60:64, :] = jnp.zeros((4, LANES), f32)


def edge_boundary(table, shared, surface_first, surface_last, source):
    position = shared[source, 56:60, :].astype(jnp.int32)
    picked = pick(table, position)
    partner = jnp.sum(shared[source, 52:56, :] * picked, axis=0, keepdims=True)
    return partner - pack_edges(surface_first, surface_last)


def own_boundary(table, index, weight, surface, out):
    offset = position_offset(out.shape[1])
    for j in range(out.shape[1] // LANES):
        cut = slice(j * LANES, (j + 1) * LANES)
        picked = pick(table, index[:, cut] + offset)
        partner = jnp.sum(weight[:, cut] * picked, axis=0, keepdims=True)
        out[:, cut] = partner - surface(j)


def couple_first(shared, index, weight, boundary, odd, even):
    section = lax.axis_index("sec")
    table = [shared[s, r : r + 1, :] for s in range(shared.shape[0]) for r in range(48, 52)]
    own_boundary(
        table, index, weight, lambda j: shared[section, 48 + j : 49 + j, :], boundary
    )
    for out, (source, start) in zip((odd, even), sent_edges()):
        for i in range(3):
            row = pl.multiple_of(2 * HALO * i + start, HALO)
            out[HALO * i : HALO * (i + 1), :] = shared[source, pl.ds(row, HALO), :]
        edge = edge_boundary(
            table, shared, shared[source, 48:49, :], shared[source, 51:52, :], source
        )
        out[24:32, :] = jnp.broadcast_to(edge, (8, LANES))


def couple_second(surfaces, shared, index, weight, boundary, odd, even):
    section = lax.axis_index("sec")
    table = [surfaces[s, r : r + 1, :] for s in range(surfaces.shape[0]) for r in range(4)]
    own_boundary(
        table, index, weight, lambda j: surfaces[section, j : j + 1, :], boundary
    )
    for out, (source, _) in zip((odd, even), sent_edges()):
        edge = edge_boundary(
            table, shared, surfaces[source, 0:1, :], surfaces[source, 3:4, :], source
        )
        out[...] = jnp.broadcast_to(edge, out.shape)


def edge_row(low, high):
    return jnp.where(lane_ids(low.shape) < HALO, high, low)


def halo_rows(odd, even, start):
    low, high = sides(odd, even, start, HALO)
    return jnp.concatenate([high, low], axis=0)


def turned(x):
    x = x.astype(f32)
    return [x[:, j * LANES : (j + 1) * LANES].T for j in range(x.shape[1] // LANES)]


def advance(field, rates, constant, right, alive):
    count = field.shape[0]
    live = alive[...] > 0.0
    for _ in range(SUBS):
        near = pltpu.roll(field, 1, 0) + pltpu.roll(field, count - 1, 0)
        spread = field + rates * (near - 2.0 * field)
        stepped = matmul(left_operand(spread), right) + constant
        field = jnp.where(live, stepped, field)
    return field


def forcing(response, boundary, edge, tendency):
    count = boundary.shape[1] // LANES
    rows = [boundary[:, j * LANES : (j + 1) * LANES] for j in range(count)]
    rows += [edge, jnp.zeros((7 - count, LANES), f32)]
    values = jnp.concatenate(rows, axis=0).T
    parts = [values[:, j : j + 1] * response for j in range(count)]
    parts.append(values[: 2 * HALO, count : count + 1] * response)
    return jnp.concatenate(parts, axis=0) + tendency


def one_hot(listed, columns):
    return jnp.concatenate(
        [
            jnp.where(listed[:, m : m + 1] == lane_ids((listed.shape[0], columns)), 1.0, 0.0)
            for m in range(listed.shape[1])
        ],
        axis=0,
    ).astype(bf16)


def chosen(field, hits):
    high, low = halves(field)
    both = matmul(hits, jnp.concatenate([high, low], axis=1))
    levels = field.shape[1]
    both = both[:, :levels] + both[:, levels:]
    tiles = hits.shape[0] // 4
    return [both[m * tiles : (m + 1) * tiles] for m in range(4)]


def place(parcels, period, picked):
    slots = len(picked)
    part = picked[0].shape[0] // PARTS
    width = PARTS * STEPS * slots
    for m, rows in enumerate(picked):
        for o in range(PARTS):
            first = (o * STEPS + period) * slots + m
            parcels[pl.ds(first, part, stride=width), :] = rows[o * part : (o + 1) * part]


def step_first(
    state, tendency, diffusion, right, response, alive, boundary, odd, even,
    window, rates_out, forcing_out, surface,
):
    rates = jnp.concatenate(turned(diffusion[...]) + [halo_rows(odd, even, 8)], axis=0)
    tend = jnp.concatenate(turned(tendency[...]) + [halo_rows(odd, even, 16)], axis=0)
    field = jnp.concatenate(turned(state[...]) + [halo_rows(odd, even, 0)], axis=0)
    edge = edge_row(*sides(odd, even, 24, 1))
    constant = forcing(response[0:1, :], boundary, edge, tend)
    rates_out[...] = rates
    forcing_out[...] = tend
    field = advance(field, rates, constant, right[...], alive)
    window[...] = field
    for j in range(surface.shape[0]):
        block = field[j * LANES : (j + 1) * LANES].T
        surface[j : j + 1, :] = block[block.shape[0] - 1 :, :]


def step_second(
    window, rates, tend, right, response, alive, hits, boundary, odd, even, earlier,
    last, parcels,
):
    edge = edge_row(*sides(odd, even, 0, 1))
    constant = forcing(response[0:1, :], boundary, edge, tend[...])
    field = advance(window[...], rates[...], constant, right[...], alive)
    own = field[: last.shape[0]]
    last[...] = own
    parcels[...] = earlier[...]
    place(parcels, 1, chosen(own, hits[...]))


def finish(last, final):
    for j in range(final.shape[1] // LANES):
        cut = slice(j * LANES, (j + 1) * LANES)
        final[:, cut] = last[cut, :].T


def ready_first(active, mixing, coupling, right, response, alive):
    right[...] = right_operand(mixing[...].T)
    response[...] = jnp.broadcast_to(coupling[...], response.shape)
    row = lax.broadcasted_iota(jnp.int32, alive.shape, 0)
    columns = alive.shape[0] - 2 * HALO
    column = jnp.where(row < columns, row, row - columns)
    column = jnp.where(row < columns + HALO, column, row - 2 * HALO)
    alive[...] = jnp.where(column < active[lax.axis_index("sec")], 1.0, 0.0)


def ready_second(
    listed, window, lists, mirrored, refraction, abel, hits, parcels, spread, right, right_abel
):
    columns = hits.shape[1]
    slots = listed.shape[1]
    places = jnp.concatenate([listed[p] for p in range(STEPS)], axis=0).T
    place(parcels, 0, chosen(window[0:columns, :], one_hot(places[:, :slots], columns)))
    hits[...] = one_hot(places[:, slots : 2 * slots], columns)
    right[...] = right_operand(refraction[...])
    right_abel[...] = right_operand(abel[...])
    occultations, width = spread.shape[2], spread.shape[3] // 3
    ranks = lists.shape[0] // (2 * STEPS)
    part = width // 4
    here = jnp.where(lax.axis_index("tile") >= part, 1, 0)
    position = lane_ids((occultations, width))
    for o in range(PARTS):
        owned = jnp.where(here == o, lists[...], mirrored[...])
        for p in range(STEPS):
            slot = owned[p * ranks : (p + 1) * ranks].astype(jnp.int32)
            live = owned[(STEPS + p) * ranks : (STEPS + p + 1) * ranks].T
            source = (slot >> 2) - here * part
            inside = (source >= 0) & (source < part)
            key = jnp.where(inside, (slot & 3) * part + source, -1).T
            total = jnp.zeros((occultations, width), f32)
            for k in range(ranks):
                hit = key[:, k : k + 1] == position
                total = total + jnp.where(hit, live[:, k : k + 1], 0.0)
            spread[o, p] = left_operand(total)


def project(arrived, spread, refraction, kept, sent):
    occultations, width = spread.shape[2:]
    part = width // 12
    profiles = []
    for o in range(PARTS):
        for p in range(STEPS):
            first = 4 * (o * STEPS + p)
            values = jnp.concatenate(
                [
                    arrived[pl.ds(first + m, part, stride=4 * PARTS * STEPS), :]
                    for m in range(4)
                ],
                axis=0,
            )
            profiles.append(matmul(spread[o, p], right_operand(values)))
    profile = jnp.concatenate(profiles, axis=0)
    projected = matmul(left_operand(profile), refraction[...])
    pairs = kept.shape[0] // PARTS
    rows = occultations // (2 * pairs)
    first_core = lax.rem(lax.axis_index("sec"), 2) == 0
    for o in range(PARTS):
        for p in range(STEPS):
            for pair in range(pairs):
                start = (o * STEPS + p) * occultations + 2 * pair * rows
                low = projected[start : start + rows]
                high = projected[start + rows : start + 2 * rows]
                target = (pair * PARTS + o, slice(p * rows, (p + 1) * rows))
                kept[target] = jnp.where(first_core, low, high)
                sent[target] = jnp.where(first_core, high, low)


def depart(received, abel, observed, out):
    total = received[0]
    for s in range(1, received.shape[0]):
        total = total + received[s]
    bending = matmul(left_operand(total), abel[...])
    steps, rows, _ = observed.shape
    for p in range(steps):
        out[p] = observed[p] - bending[p * rows : (p + 1) * rows, :]


def shards(
    state,
    tendency,
    diffusion,
    mixing,
    coupling,
    remap_index,
    remap_weight,
    active_cols,
    send_cols,
    occ_slot,
    occ_weight,
    occ_count,
    refraction,
    abel_matrix,
    observed,
):
    sections = lax.axis_size("sec")
    tiles = lax.axis_size("tile")
    levels, columns = state.shape[1:]
    rows, heights = observed.shape[1:]
    width = columns + 2 * HALO
    half = sections // 2
    part = tiles // PARTS
    ranks, owned = occ_slot.shape[2:]
    swaps = ([], [])
    for s in range(sections):
        for t in range(tiles):
            target = ((s + half) % sections if t == tiles - 1 else s) * tiles + (t + 1) % tiles
            swaps[t % 2].extend([(s * tiles + t, target), (target, s * tiles + t)])
    above_even, above_odd = swaps
    listed = jnp.transpose(send_cols[:, 0, 0], (0, 2, 1))
    index, weight = remap_index[0], remap_weight[0]
    shape = jax.ShapeDtypeStruct
    after = lax.optimization_barrier

    edges, lists = call(
        prepare,
        (shape((64, LANES), f32), shape((2 * STEPS * ranks, owned), f32)),
        *(
            pltpu.with_memory_space_constraint(x, pltpu.HBM)
            for x in (
                state[0], tendency[0], diffusion[0], index, weight,
                occ_slot[:, 0], occ_weight[:, 0], occ_count[:, 0],
            )
        ),
        space=pltpu.HBM,
        scratch=[pltpu.VMEM((levels, LANES), f32)] * 2
        + [pltpu.VMEM((levels, LANES), bf16)] * 4
        + [
            pltpu.VMEM((8, columns), f32),
            pltpu.VMEM(index.shape, jnp.int32),
            pltpu.VMEM(weight.shape, f32),
            pltpu.VMEM((STEPS, ranks, owned), jnp.int32),
            pltpu.VMEM((STEPS, ranks, owned), f32),
            pltpu.VMEM((STEPS, owned), jnp.int32),
            pltpu.SemaphoreType.DMA((12,)),
        ],
    )
    mirrored = lax.ppermute(lists, "tile", [(t, (t + part) % tiles) for t in range(tiles)])
    shared = lax.all_gather(edges, "sec", axis=0, tiled=False)
    shared, mirrored = after((shared, mirrored))
    boundary, odd, even = call(
        couple_first,
        (shape((1, columns), f32), shape((32, LANES), f32), shape((32, LANES), f32)),
        shared, index, weight,
    )
    odd = lax.ppermute(odd, AXES, above_odd)
    even = lax.ppermute(even, AXES, above_even)
    mixing_row, _ = after((mixing[0], boundary))
    right, response, alive = call(
        ready_first,
        (
            shape((3 * levels, levels), bf16),
            shape((8, levels), f32),
            shape((width, levels), f32),
        ),
        active_cols, mixing_row, coupling,
    )
    window, rates, tend, surface = call(
        step_first,
        (
            shape((width, levels), f32),
            shape((width, levels), f32),
            shape((width, levels), f32),
            shape((columns // LANES, LANES), f32),
        ),
        state[0], tendency[0], diffusion[0], right, response, alive, boundary, odd, even,
    )
    surfaces = lax.all_gather(surface, "sec", axis=0, tiled=False)
    boundary, odd, even = call(
        couple_second,
        (shape((1, columns), f32), shape((8, LANES), f32), shape((8, LANES), f32)),
        surfaces, shared, index, weight,
    )
    odd = lax.ppermute(odd, AXES, above_odd)
    even = lax.ppermute(even, AXES, above_even)
    mirrored, _ = after((mirrored, boundary))
    hits, parcels, spread, refract, bend = call(
        ready_second,
        (
            shape((4 * tiles, columns), bf16),
            shape((8 * tiles, levels), f32),
            shape((PARTS, STEPS, owned, 12 * part), bf16),
            shape((3 * levels, levels), bf16),
            shape((3 * levels, heights), bf16),
        ),
        listed, window, lists, mirrored, refraction[0], abel_matrix,
    )
    last, parcels = call(
        step_second,
        (shape((columns, levels), f32), shape((8 * tiles, levels), f32)),
        window, rates, tend, right, response, alive, hits, boundary, odd, even, parcels,
    )
    parcels, spread, refract, bend = after((parcels, spread, refract, bend))
    arrived = lax.all_to_all(
        parcels.reshape(part, 8 * PARTS, levels),
        "tile",
        split_axis=0,
        concat_axis=0,
        axis_index_groups=[[o * part + i for i in range(part)] for o in range(PARTS)],
        tiled=True,
    )
    block = shape((half * PARTS, STEPS * rows, levels), f32)
    kept, sent = call(
        project, (block, block), arrived.reshape(8 * PARTS * part, levels), spread, refract
    )
    got = lax.ppermute(sent, "sec", [(s, s ^ 1) for s in range(sections)])
    last, _ = after((last, kept))
    final = call(finish, shape((levels, columns), f32), last)
    got, final = after((got, final))
    received = lax.all_to_all(
        kept + got,
        AXES,
        split_axis=0,
        concat_axis=0,
        axis_index_groups=[
            [(2 * z + core) * tiles + o * part + i for z in range(half) for o in range(PARTS)]
            for core in range(2)
            for i in range(part)
        ],
        tiled=True,
    )
    departures = call(
        depart, shape((STEPS, rows, heights), f32), received, bend, observed
    )
    return (final[None], departures)


def solution(mesh):
    return jax.shard_map(
        shards,
        mesh=mesh,
        in_specs=(
            P("sec", None, "tile"),
            P("sec", None, "tile"),
            P("sec", None, "tile"),
            P("sec", None, None),
            P("sec", None),
            P("sec", None, "tile"),
            P("sec", None, "tile"),
            P(),
            P(None, "sec", "tile", None, None),
            P(None, "sec", None, "tile"),
            P(None, "sec", None, "tile"),
            P(None, "sec", "tile"),
            P("sec", None, None),
            P(),
            P(None, ("sec", "tile"), None),
        ),
        out_specs=(P("sec", None, "tile"), P(None, ("sec", "tile"), None)),
        check_vma=False,
    )
```

```python
import jax
import jax.numpy as jnp
from jax import lax
from jax.experimental import pallas as pl
from jax.experimental.pallas import tpu as pltpu
from jax.sharding import PartitionSpec as P

SUBS = 4
STEPS = 2
PARTS = 2
HALO = 8
LANES = 128
AXES = ("sec", "tile")
f32 = jnp.float32
bf16 = jnp.bfloat16


def call(body, outs, *args, scratch=(), space=pltpu.VMEM):
    in_specs = [
        pl.BlockSpec(memory_space=pltpu.SMEM if a.ndim == 1 else space) for a in args
    ]
    single = not isinstance(outs, (tuple, list))
    specs = pl.BlockSpec(memory_space=pltpu.VMEM)
    return pl.pallas_call(
        body,
        out_shape=outs if single else tuple(outs),
        in_specs=in_specs,
        out_specs=specs if single else tuple(specs for _ in outs),
        scratch_shapes=list(scratch),
        compiler_params=pltpu.CompilerParams(vmem_limit_bytes=40 * 2**20),
    )(*args)


def halves(x):
    high = x.astype(bf16)
    return high, (x - high.astype(f32)).astype(bf16)


def left_operand(x):
    high, low = halves(x)
    return jnp.concatenate([high, high, low], axis=1)


def right_operand(x):
    high, low = halves(x)
    return jnp.concatenate([high, low, high], axis=0)


def matmul(left, right):
    return jnp.dot(left, right, preferred_element_type=f32)


def pick(table, position):
    lane = position & (LANES - 1)
    row = position >> 7
    out = jnp.zeros(position.shape, f32)
    for r, values in enumerate(table):
        source = jnp.broadcast_to(values, position.shape)
        found = jnp.take_along_axis(source, lane, axis=1, mode="promise_in_bounds")
        out = jnp.where(row == r, found, out)
    return out


def position_offset(columns):
    ocean = lax.axis_size("sec") - 1
    return jnp.where(lax.axis_index("sec") == ocean, 0, ocean * columns)


def edge_sources():
    section, tile = lax.axis_index("sec"), lax.axis_index("tile")
    sections = lax.axis_size("sec")
    other = section + sections // 2
    other = jnp.where(other >= sections, other - sections, other)
    last = lax.axis_size("tile") - 1
    return jnp.where(tile == last, other, section), jnp.where(tile == 0, other, section)


def even_tile():
    return lax.rem(lax.axis_index("tile"), 2) == 0


def sent_edges():
    up, down = edge_sources()
    even = even_tile()
    return (
        (jnp.where(even, down, up), jnp.where(even, 0, HALO)),
        (jnp.where(even, up, down), jnp.where(even, HALO, 0)),
    )


def sides(odd, even, start, rows):
    first, second = odd[start : start + rows, :], even[start : start + rows, :]
    here = even_tile()
    return jnp.where(here, first, second), jnp.where(here, second, first)


def lane_ids(shape):
    return lax.broadcasted_iota(jnp.int32, shape, len(shape) - 1)


def pack_edges(first, last):
    lane = lane_ids(first.shape)
    return jnp.where(lane < HALO, first, pltpu.roll(last, 2 * HALO, 1))


def prepare(state, tendency, diffusion, index, weight, out, *scratch):
    levels, columns = state.shape
    tail = columns - LANES
    *ends, bottom, indices, weights, sems = scratch
    pairs = []
    for ref, head, back in zip((state, diffusion, tendency), ends[::2], ends[1::2]):
        pairs.append((ref.at[:, pl.ds(0, LANES)], head))
        pairs.append((ref.at[:, pl.ds(tail, LANES)], back))
    pairs.append((state.at[pl.ds(levels - 8, 8), :], bottom))
    pairs.append((index, indices))
    pairs.append((weight, weights))
    copies = [
        pltpu.make_async_copy(source, target, sems.at[i])
        for i, (source, target) in enumerate(pairs)
    ]
    for copy in copies:
        copy.start()
    for copy in copies:
        copy.wait()
    block = jnp.zeros((levels, LANES), f32)
    lane = lane_ids(block.shape)
    for i in range(3):
        edges = pack_edges(ends[2 * i][...].astype(f32), ends[2 * i + 1][...].astype(f32))
        if i:
            edges = pltpu.roll(edges, 2 * HALO * i, 1)
        inside = (lane >= 2 * HALO * i) & (lane < 2 * HALO * (i + 1))
        block = jnp.where(inside, edges, block)
    out[0:48, :] = block.T[0:48, :]
    for j in range(columns // LANES):
        out[48 + j : 49 + j, :] = bottom[7:8, j * LANES : (j + 1) * LANES]
    out[52:56, :] = pack_edges(weights[:, :LANES], weights[:, tail:])
    position = (indices[...] + position_offset(columns)).astype(f32)
    out[56:60, :] = pack_edges(position[:, :LANES], position[:, tail:])
    out[60:64, :] = jnp.zeros((4, LANES), f32)


def edge_boundary(table, shared, surface_first, surface_last, source):
    position = shared[source, 56:60, :].astype(jnp.int32)
    picked = pick(table, position)
    partner = jnp.sum(shared[source, 52:56, :] * picked, axis=0, keepdims=True)
    return partner - pack_edges(surface_first, surface_last)


def own_boundary(table, index, weight, surface, out):
    offset = position_offset(out.shape[1])
    for j in range(out.shape[1] // LANES):
        cut = slice(j * LANES, (j + 1) * LANES)
        picked = pick(table, index[:, cut] + offset)
        partner = jnp.sum(weight[:, cut] * picked, axis=0, keepdims=True)
        out[:, cut] = partner - surface(j)


def couple_first(
    active, shared, index, weight, slots, weights, counts, mixing, coupling,
    boundary, odd, lists, even, right, response, alive,
):
    ready_first(active, mixing, coupling, right, response, alive)
    steps, ranks, occultations = slots.shape
    for p in range(steps):
        rank = lax.broadcasted_iota(jnp.int32, (ranks, occultations), 0)
        lists[p * ranks : (p + 1) * ranks, :] = slots[p].astype(f32)
        live = jnp.where(rank < counts[p : p + 1, :], weights[p], 0.0)
        lists[(steps + p) * ranks : (steps + p + 1) * ranks, :] = live
    section = lax.axis_index("sec")
    table = [shared[s, r : r + 1, :] for s in range(shared.shape[0]) for r in range(48, 52)]
    own_boundary(
        table, index, weight, lambda j: shared[section, 48 + j : 49 + j, :], boundary
    )
    for out, (source, start) in zip((odd, even), sent_edges()):
        for i in range(3):
            row = pl.multiple_of(2 * HALO * i + start, HALO)
            out[HALO * i : HALO * (i + 1), :] = shared[source, pl.ds(row, HALO), :]
        edge = edge_boundary(
            table, shared, shared[source, 48:49, :], shared[source, 51:52, :], source
        )
        out[24:32, :] = jnp.broadcast_to(edge, (8, LANES))


def couple_second(surfaces, shared, index, weight, boundary, odd, even):
    section = lax.axis_index("sec")
    table = [surfaces[s, r : r + 1, :] for s in range(surfaces.shape[0]) for r in range(4)]
    own_boundary(
        table, index, weight, lambda j: surfaces[section, j : j + 1, :], boundary
    )
    for out, (source, _) in zip((odd, even), sent_edges()):
        edge = edge_boundary(
            table, shared, surfaces[source, 0:1, :], surfaces[source, 3:4, :], source
        )
        out[...] = jnp.broadcast_to(edge, out.shape)


def edge_row(low, high):
    return jnp.where(lane_ids(low.shape) < HALO, high, low)


def halo_rows(odd, even, start):
    low, high = sides(odd, even, start, HALO)
    return jnp.concatenate([high, low], axis=0)


def turned(x):
    x = x.astype(f32)
    return [x[:, j * LANES : (j + 1) * LANES].T for j in range(x.shape[1] // LANES)]


def advance(field, rates, constant, right, alive):
    count = field.shape[0]
    live = alive[...] > 0.0
    for _ in range(SUBS):
        near = pltpu.roll(field, 1, 0) + pltpu.roll(field, count - 1, 0)
        spread = field + rates * (near - 2.0 * field)
        stepped = matmul(left_operand(spread), right) + constant
        field = jnp.where(live, stepped, field)
    return field


def forcing(response, boundary, edge, tendency):
    count = boundary.shape[1] // LANES
    rows = [boundary[:, j * LANES : (j + 1) * LANES] for j in range(count)]
    rows += [edge, jnp.zeros((7 - count, LANES), f32)]
    values = jnp.concatenate(rows, axis=0).T
    parts = [values[:, j : j + 1] * response for j in range(count)]
    parts.append(values[: 2 * HALO, count : count + 1] * response)
    return jnp.concatenate(parts, axis=0) + tendency


def one_hot(listed, columns):
    return jnp.concatenate(
        [
            jnp.where(listed[:, m : m + 1] == lane_ids((listed.shape[0], columns)), 1.0, 0.0)
            for m in range(listed.shape[1])
        ],
        axis=0,
    ).astype(bf16)


def chosen(field, hits):
    high, low = halves(field)
    both = matmul(hits, jnp.concatenate([high, low], axis=1))
    levels = field.shape[1]
    both = both[:, :levels] + both[:, levels:]
    tiles = hits.shape[0] // 4
    return [both[m * tiles : (m + 1) * tiles] for m in range(4)]


def place(parcels, period, picked):
    slots = len(picked)
    part = picked[0].shape[0] // PARTS
    width = PARTS * STEPS * slots
    for m, rows in enumerate(picked):
        for o in range(PARTS):
            first = (o * STEPS + period) * slots + m
            parcels[pl.ds(first, part, stride=width), :] = rows[o * part : (o + 1) * part]


def step_first(
    state, tendency, diffusion, right, response, alive, boundary, odd, even,
    window, rates_out, forcing_out, surface,
):
    rates = jnp.concatenate(turned(diffusion[...]) + [halo_rows(odd, even, 8)], axis=0)
    tend = jnp.concatenate(turned(tendency[...]) + [halo_rows(odd, even, 16)], axis=0)
    field = jnp.concatenate(turned(state[...]) + [halo_rows(odd, even, 0)], axis=0)
    edge = edge_row(*sides(odd, even, 24, 1))
    constant = forcing(response[0:1, :], boundary, edge, tend)
    rates_out[...] = rates
    forcing_out[...] = tend
    field = advance(field, rates, constant, right[...], alive)
    window[...] = field
    for j in range(surface.shape[0]):
        block = field[j * LANES : (j + 1) * LANES].T
        surface[j : j + 1, :] = block[block.shape[0] - 1 :, :]


def step_second(
    window, rates, tend, right, response, alive, hits, boundary, odd, even, earlier,
    last, parcels,
):
    edge = edge_row(*sides(odd, even, 0, 1))
    constant = forcing(response[0:1, :], boundary, edge, tend[...])
    field = advance(window[...], rates[...], constant, right[...], alive)
    own = field[: last.shape[0]]
    last[...] = own
    parcels[...] = earlier[...]
    place(parcels, 1, chosen(own, hits[...]))


def finish(last, final):
    for j in range(final.shape[1] // LANES):
        cut = slice(j * LANES, (j + 1) * LANES)
        final[:, cut] = last[cut, :].T


def ready_first(active, mixing, coupling, right, response, alive):
    right[...] = right_operand(mixing[...].T)
    response[...] = jnp.broadcast_to(coupling[...], response.shape)
    row = lax.broadcasted_iota(jnp.int32, alive.shape, 0)
    columns = alive.shape[0] - 2 * HALO
    column = jnp.where(row < columns, row, row - columns)
    column = jnp.where(row < columns + HALO, column, row - 2 * HALO)
    alive[...] = jnp.where(column < active[lax.axis_index("sec")], 1.0, 0.0)


def ready_second(
    listed, window, lists, mirrored, refraction, abel, hits, parcels, spread, right, right_abel
):
    columns = hits.shape[1]
    slots = listed.shape[1]
    places = jnp.concatenate([listed[p] for p in range(STEPS)], axis=0).T
    place(parcels, 0, chosen(window[0:columns, :], one_hot(places[:, :slots], columns)))
    hits[...] = one_hot(places[:, slots : 2 * slots], columns)
    right[...] = right_operand(refraction[...])
    right_abel[...] = right_operand(abel[...])
    occultations, width = spread.shape[2], spread.shape[3] // 3
    ranks = lists.shape[0] // (2 * STEPS)
    part = width // 4
    here = jnp.where(lax.axis_index("tile") >= part, 1, 0)
    position = lane_ids((occultations, width))
    for o in range(PARTS):
        owned = jnp.where(here == o, lists[...], mirrored[...])
        for p in range(STEPS):
            slot = owned[p * ranks : (p + 1) * ranks].astype(jnp.int32)
            live = owned[(STEPS + p) * ranks : (STEPS + p + 1) * ranks].T
            source = (slot >> 2) - here * part
            inside = (source >= 0) & (source < part)
            key = jnp.where(inside, (slot & 3) * part + source, -1).T
            total = jnp.zeros((occultations, width), f32)
            for k in range(ranks):
                hit = key[:, k : k + 1] == position
                total = total + jnp.where(hit, live[:, k : k + 1], 0.0)
            spread[o, p] = left_operand(total)


def project(arrived, spread, refraction, kept, sent):
    occultations, width = spread.shape[2:]
    part = width // 12
    profiles = []
    for o in range(PARTS):
        for p in range(STEPS):
            first = 4 * (o * STEPS + p)
            values = jnp.concatenate(
                [
                    arrived[pl.ds(first + m, part, stride=4 * PARTS * STEPS), :]
                    for m in range(4)
                ],
                axis=0,
            )
            profiles.append(matmul(spread[o, p], right_operand(values)))
    profile = jnp.concatenate(profiles, axis=0)
    projected = matmul(left_operand(profile), refraction[...])
    pairs = kept.shape[0] // PARTS
    rows = occultations // (2 * pairs)
    first_core = lax.rem(lax.axis_index("sec"), 2) == 0
    for o in range(PARTS):
        for p in range(STEPS):
            for pair in range(pairs):
                start = (o * STEPS + p) * occultations + 2 * pair * rows
                low = projected[start : start + rows]
                high = projected[start + rows : start + 2 * rows]
                target = (pair * PARTS + o, slice(p * rows, (p + 1) * rows))
                kept[target] = jnp.where(first_core, low, high)
                sent[target] = jnp.where(first_core, high, low)


def depart(received, abel, observed, out):
    total = received[0]
    for s in range(1, received.shape[0]):
        total = total + received[s]
    bending = matmul(left_operand(total), abel[...])
    steps, rows, _ = observed.shape
    for p in range(steps):
        out[p] = observed[p] - bending[p * rows : (p + 1) * rows, :]


def shards(
    state,
    tendency,
    diffusion,
    mixing,
    coupling,
    remap_index,
    remap_weight,
    active_cols,
    send_cols,
    occ_slot,
    occ_weight,
    occ_count,
    refraction,
    abel_matrix,
    observed,
):
    sections = lax.axis_size("sec")
    tiles = lax.axis_size("tile")
    levels, columns = state.shape[1:]
    rows, heights = observed.shape[1:]
    width = columns + 2 * HALO
    half = sections // 2
    part = tiles // PARTS
    ranks, owned = occ_slot.shape[2:]
    swaps = ([], [])
    for s in range(sections):
        for t in range(tiles):
            target = ((s + half) % sections if t == tiles - 1 else s) * tiles + (t + 1) % tiles
            swaps[t % 2].extend([(s * tiles + t, target), (target, s * tiles + t)])
    above_even, above_odd = swaps
    listed = jnp.transpose(send_cols[:, 0, 0], (0, 2, 1))
    index, weight = remap_index[0], remap_weight[0]
    shape = jax.ShapeDtypeStruct
    after = lax.optimization_barrier

    edges = call(
        prepare,
        shape((64, LANES), f32),
        *(
            pltpu.with_memory_space_constraint(x, pltpu.HBM)
            for x in (state[0], tendency[0], diffusion[0], index, weight)
        ),
        space=pltpu.HBM,
        scratch=[pltpu.VMEM((levels, LANES), f32)] * 2
        + [pltpu.VMEM((levels, LANES), bf16)] * 4
        + [
            pltpu.VMEM((8, columns), f32),
            pltpu.VMEM(index.shape, jnp.int32),
            pltpu.VMEM(weight.shape, f32),
            pltpu.SemaphoreType.DMA((9,)),
        ],
    )
    shared = lax.all_gather(edges, "sec", axis=0, tiled=False)
    boundary, odd, lists, even, right, response, alive = call(
        couple_first,
        (
            shape((1, columns), f32),
            shape((32, LANES), f32),
            shape((2 * STEPS * ranks, owned), f32),
            shape((32, LANES), f32),
            shape((3 * levels, levels), bf16),
            shape((8, levels), f32),
            shape((width, levels), f32),
        ),
        active_cols, shared, index, weight, occ_slot[:, 0], occ_weight[:, 0], occ_count[:, 0],
        mixing[0], coupling,
    )
    odd = lax.ppermute(odd, AXES, above_odd)
    mirrored = lax.ppermute(lists, "tile", [(t, (t + part) % tiles) for t in range(tiles)])
    even = lax.ppermute(even, AXES, above_even)
    window, rates, tend, surface = call(
        step_first,
        (
            shape((width, levels), f32),
            shape((width, levels), f32),
            shape((width, levels), f32),
            shape((columns // LANES, LANES), f32),
        ),
        state[0], tendency[0], diffusion[0], right, response, alive, boundary, odd, even,
    )
    surfaces = lax.all_gather(surface, "sec", axis=0, tiled=False)
    boundary, odd, even = call(
        couple_second,
        (shape((1, columns), f32), shape((8, LANES), f32), shape((8, LANES), f32)),
        surfaces, shared, index, weight,
    )
    odd = lax.ppermute(odd, AXES, above_odd)
    even = lax.ppermute(even, AXES, above_even)
    mirrored, _ = after((mirrored, boundary))
    hits, parcels, spread, refract, bend = call(
        ready_second,
        (
            shape((4 * tiles, columns), bf16),
            shape((8 * tiles, levels), f32),
            shape((PARTS, STEPS, owned, 12 * part), bf16),
            shape((3 * levels, levels), bf16),
            shape((3 * levels, heights), bf16),
        ),
        listed, window, lists, mirrored, refraction[0], abel_matrix,
    )
    last, parcels = call(
        step_second,
        (shape((columns, levels), f32), shape((8 * tiles, levels), f32)),
        window, rates, tend, right, response, alive, hits, boundary, odd, even, parcels,
    )
    parcels, spread, refract, bend = after((parcels, spread, refract, bend))
    arrived = lax.all_to_all(
        parcels.reshape(part, 8 * PARTS, levels),
        "tile",
        split_axis=0,
        concat_axis=0,
        axis_index_groups=[[o * part + i for i in range(part)] for o in range(PARTS)],
        tiled=True,
    )
    block = shape((half * PARTS, STEPS * rows, levels), f32)
    kept, sent = call(
        project, (block, block), arrived.reshape(8 * PARTS * part, levels), spread, refract
    )
    got = lax.ppermute(sent, "sec", [(s, s ^ 1) for s in range(sections)])
    last, _ = after((last, kept))
    final = call(finish, shape((levels, columns), f32), last)
    got, final = after((got, final))
    received = lax.all_to_all(
        kept + got,
        AXES,
        split_axis=0,
        concat_axis=0,
        axis_index_groups=[
            [(2 * z + core) * tiles + o * part + i for z in range(half) for o in range(PARTS)]
            for core in range(2)
            for i in range(part)
        ],
        tiled=True,
    )
    departures = call(
        depart, shape((STEPS, rows, heights), f32), received, bend, observed
    )
    return (final[None], departures)


def solution(mesh):
    return jax.shard_map(
        shards,
        mesh=mesh,
        in_specs=(
            P("sec", None, "tile"),
            P("sec", None, "tile"),
            P("sec", None, "tile"),
            P("sec", None, None),
            P("sec", None),
            P("sec", None, "tile"),
            P("sec", None, "tile"),
            P(),
            P(None, "sec", "tile", None, None),
            P(None, "sec", None, "tile"),
            P(None, "sec", None, "tile"),
            P(None, "sec", "tile"),
            P("sec", None, None),
            P(),
            P(None, ("sec", "tile"), None),
        ),
        out_specs=(P("sec", None, "tile"), P(None, ("sec", "tile"), None)),
        check_vma=False,
    )
```
